32 devices in a mesh: dp: 16 (over z, y, core), tensor: 2 (over x).
Axes of the slice: x: 2, y: 2, z: 4, core: 2. Of those that a mesh axis runs over, the one named last changes fastest.
Arguments:
- tokens: bfloat16 [4096, 1024], P(('dp', 'tensor')), may hold values from -6 to 6
- out_cotangent: bfloat16 [4096, 1024], P(('dp', 'tensor')), may hold values from -6 to 6
- seq_lengths: int32 [16], P('dp'), may hold values from 1 to 256, 2048 in all
- norm_gain1: float32 [1024], replicated, may hold values from 0.1 to 1.9
- query_weight: bfloat16 [1024, 1024], P('dp', 'tensor'), may hold values from -0.1875 to 0.1875
- key_weight: bfloat16 [1024, 1024], P('dp', 'tensor'), may hold values from -0.1875 to 0.1875
- value_weight: bfloat16 [1024, 2048], P('dp', 'tensor'), may hold values from -0.1875 to 0.1875
- out_gate_weight: bfloat16 [1024, 2048], P('dp', 'tensor'), may hold values from -0.1875 to 0.1875
- beta_weight: bfloat16 [1024, 8], P('dp', 'tensor'), may hold values from -0.1875 to 0.1875
- decay_weight: bfloat16 [1024, 8], P('dp', 'tensor'), may hold values from -0.1875 to 0.1875
- conv_query: float32 [4, 1024], P(None, 'tensor'), may hold values from -3 to 3
- conv_key: float32 [4, 1024], P(None, 'tensor'), may hold values from -3 to 3
- conv_value: float32 [4, 2048], P(None, 'tensor'), may hold values from -3 to 3
- decay_log_rate: float32 [8], P('tensor'), may hold values from -4 to 1
- decay_bias: float32 [8], P('tensor'), may hold values from -4 to 0
- out_gain: float32 [256], replicated, may hold values from 0.1 to 1.9
- out_weight: bfloat16 [1024, 2048], P('dp', 'tensor'), may hold values from -0.25 to 0.25
- norm_gain2: float32 [1024], replicated, may hold values from 0.1 to 1.9
- ffn_gate_weight: bfloat16 [1024, 2816], P('dp', 'tensor'), may hold values from -0.1875 to 0.1875
- ffn_up_weight: bfloat16 [1024, 2816], P('dp', 'tensor'), may hold values from -0.1875 to 0.1875
- ffn_down_weight: bfloat16 [1024, 2816], P('dp', 'tensor'), may hold values from -0.109375 to 0.109375
Outputs:
- output: bfloat16 [4096, 1024], P(('dp', 'tensor'))
- grad_tokens: bfloat16 [4096, 1024], P(('dp', 'tensor'))
- grad_norm_gain1: float32 [1024], replicated
- grad_query_weight: float32 [1024, 1024], P('dp', 'tensor')
- grad_key_weight: float32 [1024, 1024], P('dp', 'tensor')
- grad_value_weight: float32 [1024, 2048], P('dp', 'tensor')
- grad_out_gate_weight: float32 [1024, 2048], P('dp', 'tensor')
- grad_beta_weight: float32 [1024, 8], P('dp', 'tensor')
- grad_decay_weight: float32 [1024, 8], P('dp', 'tensor')
- grad_conv_query: float32 [4, 1024], replicated
- grad_conv_key: float32 [4, 1024], replicated
- grad_conv_value: float32 [4, 2048], replicated
- grad_decay_log_rate: float32 [8], replicated
- grad_decay_bias: float32 [8], replicated
- grad_out_gain: float32 [256], replicated
- grad_out_weight: float32 [1024, 2048], P('dp', 'tensor')
- grad_norm_gain2: float32 [1024], replicated
- grad_ffn_gate_weight: float32 [1024, 2816], P('dp', 'tensor')
- grad_ffn_up_weight: float32 [1024, 2816], P('dp', 'tensor')
- grad_ffn_down_weight: float32 [1024, 2816], P('dp', 'tensor')
The draws below stay inside these ranges and needn't reach their ends.
Inputs may be any that keep to these rules, and one draw needn't show every extreme that they name: `seq_lengths`: the number of valid tokens of each sequence; the largest is exactly 256.
All inputs are finite; a program needn't handle non-finite values. No bound on the sum of `seq_lengths` on one device may be relied on, other than what follows from the above.
Results may differ from the reference program's by a relative error of at most 0.012.
Values may be sent and summed in bfloat16 or wider, within the bound.
No kernel may reach another device: no remote copies, remote signals or barrier semaphores. Data moves between devices by JAX's collectives and lax.ppermute only.
A program may use at most 192 MiB of HBM per device.

```python
import math
import jax
import jax.numpy as jnp
import numpy as np
from jax import lax

D = 1024
H = 8
DK = 128
DV = 256
FF = 2816
CONV = 4
GROUP = 64
LEN = 256
SEQS = 16
TOKENS = 4096
TOTAL_LEN = 2048


def with_spikes(drawn, key, source, target, shards_of, factor):
    def block_of(dim):
        return (jnp.arange(drawn.shape[dim]) // (drawn.shape[dim] // shards_of)).reshape((-1,) + (1,) * (drawn.ndim - 1 - dim))

    near = jax.random.permutation(key, shards_of)[block_of(target)]
    other_side = (block_of(target) + shards_of // 2) % shards_of
    return jnp.where((block_of(source) == near) | (block_of(source) == other_side), factor * drawn, drawn)


def block_levels(rng, dims, split, least, largest):
    level = 1.0
    for dim, blocks in split:
        heights = jax.random.uniform(jax.random.fold_in(jax.random.fold_in(rng, 6), dim), (blocks,), jnp.float32, least / len(split), largest / len(split))
        level = level * jnp.repeat(jnp.exp(heights), dims[dim] // blocks).reshape((-1,) + (1,) * (len(dims) - 1 - dim))
    return level


def profile(amount, total, limit, slope):
    portions = [(1 << 20) // math.isqrt(standing ** slope) + 1 for standing in range(2, amount + 1)]
    spare, holding = total - limit - (amount - 1), [1] * (amount - 1)
    while spare > 0:
        movable = [i for i in range(amount - 1) if holding[i] < limit]
        mass, remaining = sum([portions[i] for i in movable]), spare
        for i in movable:
            extra = min(limit - holding[i], max(1, remaining * portions[i] // mass), spare)
            holding[i] = holding[i] + extra
            spare = spare - extra
    return np.array([limit] + holding)


def ragged(rng, number_of, total, limit, lean):
    if number_of == 2:
        one = jax.random.randint(rng, (), max(1, total - limit), min(limit, total - 1) + 1)
        return jnp.stack([one, total - one])
    sizes = jnp.asarray(profile(number_of, total, limit, lean), jnp.int32)
    pairs = (number_of - 1) // 2
    donor, sink = sizes[1:1 + 2 * pairs:2], sizes[2:2 + 2 * pairs:2]
    room = jnp.minimum(donor - 1, limit - sink)
    moved = jax.random.randint(jax.random.fold_in(rng, 1), (pairs,), 0, 1 << 20) % (room + 1)
    sizes = sizes.at[1:1 + 2 * pairs:2].set(donor - moved).at[2:2 + 2 * pairs:2].set(sink + moved)
    return sizes[jax.random.permutation(jax.random.fold_in(rng, 2), number_of)]


def noise(own_key, dims, scale, limit, cuts=(), kind=jnp.bfloat16):
    level = block_levels(own_key, dims, cuts, -0.22, 0.18) if cuts else 1.0
    drawn = jax.random.normal(own_key, dims, jnp.float32) * scale * level
    return jnp.minimum(jnp.maximum(drawn, -limit), limit).astype(kind)


def heavy_noise(own_key, extent, scale, most, pieces, heavy, held_as=jnp.bfloat16):
    drawn = scale * jax.random.normal(own_key, extent, jnp.float32)
    if pieces:
        drawn = drawn * block_levels(own_key, extent, pieces, -0.22, 0.18)
    return jnp.clip(with_spikes(drawn, jax.random.fold_in(own_key, 3), *heavy), -most, most).astype(held_as)


def setup_inputs(seed: int = 0) -> dict:
    key_of = jax.random.split(jax.random.key(seed), 22)
    return {
        "tokens": heavy_noise(key_of[0], (TOKENS, D), 1.0, 6.0, ((0, 32),), (0, 1, 32, 2.75)),
        "out_cotangent": noise(key_of[1], (TOKENS, D), 1.0, 6.0, ((0, 32),)),
        "seq_lengths": ragged(key_of[2], SEQS, TOTAL_LEN, LEN, 2).astype(jnp.int32),
        "norm_gain1": jnp.clip(1.0 + 0.18 * jax.random.normal(key_of[3], (D,), jnp.float32), 0.1, 1.9),
        "query_weight": noise(key_of[4], (D, H * DK), D ** -0.5, 0.1875, ((0, 16), (1, 2))),
        "key_weight": noise(key_of[5], (D, H * DK), D ** -0.5, 0.1875, ((0, 16), (1, 2))),
        "value_weight": noise(key_of[6], (D, H * DV), D ** -0.5, 0.1875, ((0, 16), (1, 2))),
        "out_gate_weight": noise(key_of[7], (D, H * DV), D ** -0.5, 0.1875, ((0, 16), (1, 2))),
        "beta_weight": noise(key_of[8], (D, H), D ** -0.5, 0.1875, ((0, 16), (1, 2))),
        "decay_weight": noise(key_of[9], (D, H), D ** -0.5, 0.1875, ((0, 16), (1, 2))),
        "conv_query": noise(key_of[10], (CONV, H * DK), 0.5, 3.0, ((1, 2),), jnp.float32),
        "conv_key": noise(key_of[11], (CONV, H * DK), 0.5, 3.0, ((1, 2),), jnp.float32),
        "conv_value": noise(key_of[12], (CONV, H * DV), 0.5, 3.0, ((1, 2),), jnp.float32),
        "decay_log_rate": jnp.clip(-4.0 + 5.0 * jax.random.uniform(key_of[13], (H,), jnp.float32) ** block_levels(key_of[13], (H,), ((0, 2),), -0.2, 0.2), -4.0, 1.0),
        "decay_bias": jnp.clip(-4.0 + 4.0 * jax.random.uniform(key_of[14], (H,), jnp.float32) ** block_levels(key_of[14], (H,), ((0, 2),), -0.2, 0.2), -4.0, 0.0),
        "out_gain": jnp.clip(1.0 + 0.18 * jax.random.normal(key_of[15], (DV,), jnp.float32), 0.1, 1.9),
        "out_weight": noise(key_of[16], (D, H * DV), (H * DV // 4) ** -0.5, 0.25, ((0, 16), (1, 2))),
        "norm_gain2": jnp.clip(1.0 + 0.18 * jax.random.normal(key_of[17], (D,), jnp.float32), 0.1, 1.9),
        "ffn_gate_weight": noise(key_of[18], (D, FF), D ** -0.5, 0.1875, ((0, 16), (1, 2))),
        "ffn_up_weight": noise(key_of[19], (D, FF), D ** -0.5, 0.1875, ((0, 16), (1, 2))),
        "ffn_down_weight": noise(key_of[20], (D, FF), FF ** -0.5, 0.109375, ((0, 16), (1, 2))),
    }


highest = lax.Precision.HIGHEST

def plain_dot(left, right):
    return jnp.dot(left.astype(jnp.float32), right.astype(jnp.float32), preferred_element_type=jnp.float32)

def left_dot(left, right):
    return lax.dot_general(left.astype(jnp.float32), right.astype(jnp.float32), (((0,), (0,)), ((), ())), preferred_element_type=jnp.float32)

def right_dot(left, right):
    return lax.dot_general(left.astype(jnp.float32), right.astype(jnp.float32), (((1,), (1,)), ((), ())), preferred_element_type=jnp.float32)

def exact_dot(left, right):
    return jnp.dot(left, right, precision=highest)

def rms_rows(inputs, gain):
    wide_rows = inputs.astype(jnp.float32)
    inverse = lax.rsqrt(lax.optimization_barrier(jnp.mean(wide_rows * wide_rows, -1, keepdims=True)) + 1e-05)
    normed = wide_rows * inverse
    return (normed, inverse, (normed * gain).astype(jnp.bfloat16))

def rms_back(grad_rows, normed, inverse, gain):
    scaled = grad_rows * gain
    grad_in = inverse * (scaled - normed * lax.optimization_barrier(jnp.mean(scaled * normed, -1, keepdims=True)))
    return (grad_in, lax.optimization_barrier(jnp.sum(grad_rows * normed, 0)))

def causal_conv(projected, kernel):
    kernel_len = kernel.shape[0]
    summed = kernel[kernel_len - 1] * projected
    for offset in range(1, kernel_len):
        shifted = jnp.pad(projected[:-offset], ((offset, 0), (0, 0)))
        summed = summed + kernel[kernel_len - 1 - offset] * shifted
    return summed

def delta_block(state, element):
    block_query, block_key, block_value, block_beta, block_gate = element
    block_len = block_key.shape[0]
    value_dim = block_value.shape[1]
    lower_all = jnp.tril(jnp.ones((block_len, block_len), dtype=bool))
    strict_lower = jnp.tril(jnp.ones((block_len, block_len), dtype=bool), -1)
    cumulative = jnp.cumsum(block_gate)
    spread = cumulative[:, None] - cumulative[None, :]
    decays = jnp.where(lower_all, jnp.exp(jnp.where(lower_all, spread, 0.0)), 0.0)
    key_key = exact_dot(block_key, block_key.T)
    coupling = jnp.where(strict_lower, block_beta[:, None] * key_key * decays, 0.0)
    stacked = jnp.concatenate([block_beta[:, None] * block_value, (block_beta * jnp.exp(cumulative))[:, None] * block_key], axis=1)
    solved = lax.linalg.triangular_solve(coupling + jnp.eye(block_len, dtype=jnp.float32), stacked, left_side=True, lower=True, unit_diagonal=True)
    updates = solved[:, :value_dim] - exact_dot(solved[:, value_dim:], state.T)
    query_key = jnp.where(lower_all, exact_dot(block_query, block_key.T) * decays, 0.0)
    outputs = jnp.exp(cumulative)[:, None] * exact_dot(block_query, state.T) + exact_dot(query_key, updates)
    final_log = cumulative[-1]
    new_state = jnp.exp(final_log) * state + exact_dot(updates.T, block_key * jnp.exp(final_log - cumulative)[:, None])
    return (new_state, outputs)

def delta_rule(query_rows, key_rows, value_rows, beta_rows, log_gates, block_len):
    length, head_count, key_dim = key_rows.shape
    value_dim = value_rows.shape[2]
    blocks = length // block_len

    def split_heads(array):
        shaped = array.reshape((blocks, block_len) + array.shape[1:])
        return jnp.moveaxis(shaped, 2, 0)

    def one_head(head_query, head_key, head_value, head_beta, head_gate):
        start_state = jnp.zeros((value_dim, key_dim), jnp.float32)
        unused, outputs = lax.scan(delta_block, start_state, (head_query, head_key, head_value, head_beta, head_gate))
        return outputs
    per_head = jax.vmap(one_head)(split_heads(query_rows), split_heads(key_rows), split_heads(value_rows), split_heads(beta_rows), split_heads(log_gates))
    return jnp.transpose(per_head, (1, 2, 0, 3)).reshape(length, head_count, value_dim)

def mixer(proj_query, proj_key, proj_value, proj_gate, proj_beta, proj_decay, conv_query, conv_key, conv_value, decay_log_rate, decay_bias, out_gain):
    length = proj_query.shape[0]
    head_count = proj_beta.shape[1]
    query_rows = jax.nn.silu(causal_conv(proj_query, conv_query)).reshape(length, head_count, -1)
    key_rows = jax.nn.silu(causal_conv(proj_key, conv_key)).reshape(length, head_count, -1)
    value_rows = jax.nn.silu(causal_conv(proj_value, conv_value)).reshape(length, head_count, -1)
    key_dim = query_rows.shape[2]
    query_rows = query_rows * lax.rsqrt(lax.optimization_barrier(jnp.sum(query_rows * query_rows, -1, keepdims=True)) + 1e-06) * key_dim ** (-0.5)
    key_rows = key_rows * lax.rsqrt(lax.optimization_barrier(jnp.sum(key_rows * key_rows, -1, keepdims=True)) + 1e-06)
    beta_rows = jax.nn.sigmoid(proj_beta)
    log_gates = -jnp.exp(decay_log_rate) * jax.nn.softplus(proj_decay + decay_bias)
    mixed = delta_rule(query_rows, key_rows, value_rows, beta_rows, log_gates, GROUP)
    inverse = lax.rsqrt(lax.optimization_barrier(jnp.mean(mixed * mixed, -1, keepdims=True)) + 1e-05)
    gated = mixed * inverse * out_gain * jax.nn.silu(proj_gate.reshape(length, head_count, -1))
    return gated.reshape(length, -1)

def reference(tokens, out_cotangent, seq_lengths, norm_gain1, query_weight, key_weight, value_weight, out_gate_weight, beta_weight, decay_weight, conv_query, conv_key, conv_value, decay_log_rate, decay_bias, out_gain, out_weight, norm_gain2, ffn_gate_weight, ffn_up_weight, ffn_down_weight):
    seq_count = seq_lengths.shape[0]
    model_dim = tokens.shape[1]
    token_blocks = tokens.reshape(seq_count, -1, model_dim)
    cot_blocks = out_cotangent.reshape(seq_count, -1, model_dim)
    proj_weights = (query_weight, key_weight, value_weight, out_gate_weight, beta_weight, decay_weight)

    def one_sequence(summed_totals, element):
        seq_tokens, seq_cot, seq_length = element
        positions = jnp.arange(seq_tokens.shape[0], dtype=jnp.int32)
        valid = positions < seq_length
        row_mask = valid.astype(jnp.float32)[:, None]
        half_mask = valid.astype(jnp.bfloat16)[:, None]
        normed1, inverse1, hidden1 = rms_rows(seq_tokens, norm_gain1)
        projections = tuple((plain_dot(hidden1, weight) for weight in proj_weights))
        mixed_out, pullback = jax.vjp(mixer, projections[0], projections[1], projections[2], projections[3], projections[4], projections[5], conv_query, conv_key, conv_value, decay_log_rate, decay_bias, out_gain)
        mixed_half = mixed_out.astype(jnp.bfloat16)
        residual = seq_tokens.astype(jnp.float32) + right_dot(mixed_half, out_weight)
        normed2, inverse2, hidden2 = rms_rows(residual, norm_gain2)
        gate_pre = plain_dot(hidden2, ffn_gate_weight)
        up_pre = plain_dot(hidden2, ffn_up_weight)
        gate_act = jax.nn.silu(gate_pre)
        inner_act = (gate_act * up_pre).astype(jnp.bfloat16)
        output = (row_mask * (residual + right_dot(inner_act, ffn_down_weight))).astype(jnp.bfloat16)
        grad_whole = seq_cot * half_mask
        grad_inner = plain_dot(grad_whole, ffn_down_weight)
        down_weight_gradient = left_dot(grad_whole, inner_act)
        sigma_gate = jax.nn.sigmoid(gate_pre)
        grad_gate_pre = (grad_inner * up_pre * sigma_gate * (1.0 + gate_pre * (1.0 - sigma_gate))).astype(jnp.bfloat16)
        grad_up_pre = (grad_inner * gate_act).astype(jnp.bfloat16)
        gate_weight_gradient = left_dot(hidden2, grad_gate_pre)
        up_weight_gradient = left_dot(hidden2, grad_up_pre)
        grad_hidden2 = right_dot(grad_gate_pre, ffn_gate_weight) + right_dot(grad_up_pre, ffn_up_weight)
        grad_normed2, second_gain_gradient = rms_back(grad_hidden2, normed2, inverse2, norm_gain2)
        grad_residual = row_mask * seq_cot.astype(jnp.float32) + grad_normed2
        grad_half = grad_residual.astype(jnp.bfloat16)
        grad_mixed = plain_dot(grad_half, out_weight)
        output_weight_gradient = left_dot(grad_half, mixed_half)
        mixer_gradient_list = pullback(grad_mixed)
        grad_projs = tuple((member.astype(jnp.bfloat16) for member in mixer_gradient_list[:6]))
        projection_gradients = tuple((left_dot(hidden1, member) for member in grad_projs))
        grad_hidden1 = right_dot(grad_projs[0], proj_weights[0])
        for index_pos in range(1, 6):
            grad_hidden1 = grad_hidden1 + right_dot(grad_projs[index_pos], proj_weights[index_pos])
        grad_normed1, first_gain_gradient = rms_back(grad_hidden1, normed1, inverse1, norm_gain1)
        grad_tokens = (grad_residual + grad_normed1).astype(jnp.bfloat16)
        partial_terms = (first_gain_gradient, projection_gradients[0], projection_gradients[1], projection_gradients[2], projection_gradients[3], projection_gradients[4], projection_gradients[5], mixer_gradient_list[6], mixer_gradient_list[7], mixer_gradient_list[8], mixer_gradient_list[9], mixer_gradient_list[10], mixer_gradient_list[11], output_weight_gradient, second_gain_gradient, gate_weight_gradient, up_weight_gradient, down_weight_gradient)
        summed_totals = tuple((running_total + partial_term for running_total, partial_term in zip(summed_totals, partial_terms)))
        return (summed_totals, (output, grad_tokens))
    shapes_of = (norm_gain1, query_weight, key_weight, value_weight, out_gate_weight, beta_weight, decay_weight, conv_query, conv_key, conv_value, decay_log_rate, decay_bias, out_gain, out_weight, norm_gain2, ffn_gate_weight, ffn_up_weight, ffn_down_weight)
    initial = tuple((jnp.zeros(member.shape, jnp.float32) for member in shapes_of))
    summed_totals, (outputs, grad_rows) = lax.scan(one_sequence, initial, (token_blocks, cot_blocks, seq_lengths))
    return (outputs.reshape(-1, model_dim), grad_rows.reshape(-1, model_dim), summed_totals[0], summed_totals[1], summed_totals[2], summed_totals[3], summed_totals[4], summed_totals[5], summed_totals[6], summed_totals[7], summed_totals[8], summed_totals[9], summed_totals[10], summed_totals[11], summed_totals[12], summed_totals[13], summed_totals[14], summed_totals[15], summed_totals[16], summed_totals[17])
```

```python
import functools

import jax
import jax.numpy as jnp
from jax import lax
from jax.experimental import pallas as pl
from jax.experimental.pallas import tpu as pltpu
from jax.sharding import PartitionSpec as P

SUB = 128
UNROLLED_CHIPS = 16
bf16 = jnp.bfloat16
f32 = jnp.float32


def dims_of(kind):
    return {
        "nn": (((1,), (0,)), ((), ())),
        "nt": (((1,), (1,)), ((), ())),
        "tn": (((0,), (0,)), ((), ())),
    }[kind]


def dot1(left, right, kind="nn"):
    return lax.dot_general(left, right, dims_of(kind), preferred_element_type=f32)


def cut(array):
    high = array.astype(bf16)
    return (high, (array - high.astype(f32)).astype(bf16))


def dot3(left, right, kind="nn"):
    return (
        dot1(left[0], right[0], kind)
        + dot1(left[0], right[1], kind)
        + dot1(left[1], right[0], kind)
    )


def shift_down(array, amount):
    if amount == 0:
        return array
    rows = lax.broadcasted_iota(jnp.int32, array.shape, 0)
    return jnp.where(rows >= amount, pltpu.roll(array, amount, 0), 0.0)


def shift_up(array, amount):
    if amount == 0:
        return array
    length = array.shape[0]
    rows = lax.broadcasted_iota(jnp.int32, array.shape, 0)
    return jnp.where(rows < length - amount, pltpu.roll(array, length - amount, 0), 0.0)


def conv_rows(projected, kernel):
    taps = kernel.shape[0]
    summed = kernel[taps - 1 : taps] * projected
    for offset in range(1, taps):
        tap = taps - 1 - offset
        summed = summed + kernel[tap : tap + 1] * shift_down(projected, offset)
    return summed


def conv_back(grad_conv, projected, kernel):
    taps = kernel.shape[0]
    grad_proj = kernel[taps - 1 : taps] * grad_conv
    for offset in range(1, taps):
        tap = taps - 1 - offset
        grad_proj = grad_proj + kernel[tap : tap + 1] * shift_up(grad_conv, offset)
    terms = []
    for tap in range(taps):
        moved = shift_down(projected, taps - 1 - tap)
        terms.append(jnp.sum(grad_conv * moved, 0, keepdims=True))
    return grad_proj, jnp.concatenate(terms, 0)


def silu_slope(values, sigma):
    return sigma * (1.0 + values * (1.0 - sigma))


def gate_rows(small, lanes_ref, heads):
    lane = lax.broadcasted_iota(jnp.int32, small.shape, 1)
    rate = jnp.exp(lanes_ref[0:1, :])
    shifted = small + lanes_ref[1:2, :]
    soft = jnp.maximum(shifted, 0.0) + jnp.log1p(jnp.exp(-jnp.abs(shifted)))
    gates = jnp.where(lane >= heads, -rate * soft, 0.0)
    slope = jnp.where(lane >= heads, -rate * jax.nn.sigmoid(shifted), 0.0)
    return jax.nn.sigmoid(small), gates, slope


def sum_gates(gates):
    length = gates.shape[0]
    row = lax.broadcasted_iota(jnp.int32, (length, length), 0)
    col = lax.broadcasted_iota(jnp.int32, (length, length), 1)
    lower = (row >= col).astype(f32)
    upper = (row <= col).astype(f32)
    kwargs = dict(precision=lax.Precision.HIGHEST, preferred_element_type=f32)
    by_row = lax.dot_general(lower, gates, dims_of("nn"), **kwargs)
    by_col = lax.dot_general(gates, upper, dims_of("tn"), **kwargs)
    return by_row, by_col


def lane_pick(array, index):
    lane = lax.broadcasted_iota(jnp.int32, array.shape, 1)
    return jnp.sum(jnp.where(lane == index, array, 0.0), 1, keepdims=True)


def row_pick(array, index):
    row = lax.broadcasted_iota(jnp.int32, array.shape, 0)
    return jnp.sum(jnp.where(row == index, array, 0.0), 0, keepdims=True)


def decay_square(cum_col, cum_row):
    length = cum_col.shape[0]
    row = lax.broadcasted_iota(jnp.int32, (length, length), 0)
    col = lax.broadcasted_iota(jnp.int32, (length, length), 1)
    keep = row >= col
    square = jnp.where(keep, jnp.exp(jnp.where(keep, cum_col - cum_row, 0.0)), 0.0)
    return square, keep, row > col


def unit_rows(raw, kernel):
    conv = conv_rows(raw, kernel)
    sigma = jax.nn.sigmoid(conv)
    act = conv * sigma
    inverse = lax.rsqrt(jnp.sum(act * act, -1, keepdims=True) + 1e-06)
    return conv, sigma, act, inverse


def forward_kernel(
    heads, per_step, key_dim, value_dim,
    query_ref, key_ref, value_ref, gate_ref, small_ref, lanes_ref,
    conv_query_ref, conv_key_ref, conv_value_ref, gain_ref,
    half_ref, mixed_ref, update_ref, inverse_ref,
):
    step = pl.program_id(0)
    length = query_ref.shape[0]
    blocks = length // SUB
    beta_all, gates_all, _ = gate_rows(small_ref[...], lanes_ref, heads)
    cum_all, cum_rows = sum_gates(gates_all)
    sub_row = lax.broadcasted_iota(jnp.int32, (SUB, SUB), 0)
    sub_col = lax.broadcasted_iota(jnp.int32, (SUB, SUB), 1)
    state = []
    for local in range(per_step):
        head = step * per_step + local
        kcut = slice(local * key_dim, (local + 1) * key_dim)
        vcut = slice(local * value_dim, (local + 1) * value_dim)
        _, _, query_act, query_inv = unit_rows(query_ref[:, kcut], conv_query_ref[:, kcut])
        query = query_act * query_inv * key_dim ** (-0.5)
        _, _, key_act, key_inv = unit_rows(key_ref[:, kcut], conv_key_ref[:, kcut])
        key = key_act * key_inv
        value_conv = conv_rows(value_ref[:, vcut], conv_value_ref[:, vcut])
        value = value_conv * jax.nn.sigmoid(value_conv)
        beta = lane_pick(beta_all, head)
        decay, keep, strict = decay_square(
            lane_pick(cum_all, heads + head), row_pick(cum_rows, heads + head)
        )
        key_parts = cut(key)
        coupling = jnp.where(strict, beta * dot3(key_parts, key_parts, "nt") * decay, 0.0)
        mix = dot3(cut(query), key_parts, "nt") * decay
        state.append((coupling, mix, beta * value))
    inverses = []
    for coupling, _, _ in state:
        parts = []
        for block in range(blocks):
            span = slice(block * SUB, (block + 1) * SUB)
            parts.append(coupling[span, span])
        inverses.append(parts)
    squares = [[part for part in parts] for parts in inverses]
    eye = (sub_row == sub_col).astype(f32)
    size = 1
    current = [[None] * blocks for _ in state]
    while size < SUB:
        member = ((sub_row // (2 * size)) == (sub_col // (2 * size))) & (
            (sub_row // size) != (sub_col // size)
        )
        for h in range(per_step):
            for block in range(blocks):
                cross = jnp.where(member, squares[h][block], 0.0)
                if size == 1:
                    current[h][block] = eye - cross
                else:
                    now = cut(current[h][block])
                    inner = dot3(cut(cross), now)
                    current[h][block] = current[h][block] - dot3(now, cut(inner))
        size = 2 * size
    for local in range(per_step):
        vcut = slice(local * value_dim, (local + 1) * value_dim)
        coupling, mix, target = state[local]
        solved = []
        for block in range(blocks):
            span = slice(block * SUB, (block + 1) * SUB)
            rest = target[span]
            for before in range(block):
                past = slice(before * SUB, (before + 1) * SUB)
                rest = rest - dot3(cut(coupling[span, past]), cut(solved[before]))
            solved.append(dot3(cut(current[local][block]), cut(rest)))
            inverse_ref[local, block] = current[local][block]
        updates = jnp.concatenate(solved, 0)
        mixed = dot3(cut(mix), cut(updates))
        update_ref[:, vcut] = updates
        mixed_ref[:, vcut] = mixed
        inverse = lax.rsqrt(jnp.mean(mixed * mixed, -1, keepdims=True) + 1e-05)
        gate = gate_ref[:, vcut]
        half_ref[:, vcut] = (
            mixed * inverse * gain_ref[...] * (gate * jax.nn.sigmoid(gate))
        ).astype(bf16)


def unit_back(grad, conv, sigma, act, inverse, scale):
    inner = jnp.sum(grad * act, -1, keepdims=True)
    grad_act = scale * inverse * (grad - act * (inverse * inverse) * inner)
    return grad_act * silu_slope(conv, sigma)


def backward_kernel(
    heads, per_step, key_dim, value_dim, offsets,
    query_ref, key_ref, value_ref, gate_ref, small_ref, lanes_ref,
    conv_query_ref, conv_key_ref, conv_value_ref, gain_ref,
    mixed_ref, update_ref, inverse_ref, grad_ref,
    grads_ref, conv_query_out, conv_key_out, conv_value_out, gain_out, lanes_out,
    beta_acc, gate_acc,
):
    step = pl.program_id(0)
    length = query_ref.shape[0]
    blocks = length // SUB
    small = small_ref[...]
    beta_all, gates_all, slope_all = gate_rows(small, lanes_ref, heads)
    cum_all, cum_rows = sum_gates(gates_all)
    lane = lax.broadcasted_iota(jnp.int32, small.shape, 1)
    upper = (
        lax.broadcasted_iota(jnp.int32, (length, length), 0)
        <= lax.broadcasted_iota(jnp.int32, (length, length), 1)
    ).astype(bf16)

    @pl.when(step == 0)
    def _():
        beta_acc[...] = jnp.zeros_like(beta_acc)
        gate_acc[...] = jnp.zeros_like(gate_acc)
        gain_out[...] = jnp.zeros_like(gain_out)

    for local in range(per_step):
        head = step * per_step + local
        kcut = slice(local * key_dim, (local + 1) * key_dim)
        vcut = slice(local * value_dim, (local + 1) * value_dim)
        scale = key_dim ** (-0.5)
        query_raw = query_ref[:, kcut]
        key_raw = key_ref[:, kcut]
        value_raw = value_ref[:, vcut]
        query_conv, query_sigma, query_act, query_inv = unit_rows(
            query_raw, conv_query_ref[:, kcut]
        )
        query = query_act * query_inv * scale
        key_conv, key_sigma, key_act, key_inv = unit_rows(key_raw, conv_key_ref[:, kcut])
        key = key_act * key_inv
        value_conv = conv_rows(value_raw, conv_value_ref[:, vcut])
        value_sigma = jax.nn.sigmoid(value_conv)
        value = value_conv * value_sigma
        mixed = mixed_ref[:, vcut]
        inverse = lax.rsqrt(jnp.mean(mixed * mixed, -1, keepdims=True) + 1e-05)
        gate = gate_ref[:, vcut]
        gate_sigma = jax.nn.sigmoid(gate)
        gain = gain_ref[...]
        normed = mixed * inverse
        grad_out = grad_ref[:, vcut]
        through = grad_out * normed
        grad_gate = through * gain * silu_slope(gate, gate_sigma)
        swish = gate * gate_sigma
        gain_out[0:1, :] += jnp.sum(through * swish, 0, keepdims=True)
        grad_normed = grad_out * gain * swish
        grad_mixed = inverse * (
            grad_normed - normed * jnp.mean(grad_normed * normed, -1, keepdims=True)
        )
        beta = lane_pick(beta_all, head)
        decay, keep, strict = decay_square(
            lane_pick(cum_all, heads + head), row_pick(cum_rows, heads + head)
        )
        key_parts = cut(key)
        query_parts = cut(query)
        pair = dot3(key_parts, key_parts, "nt") * decay
        coupling = jnp.where(strict, beta * pair, 0.0)
        mix = dot3(query_parts, key_parts, "nt") * decay
        updates = cut(update_ref[:, vcut])
        grad_parts = cut(grad_mixed)
        grad_mix = jnp.where(keep, dot3(grad_parts, updates, "nt"), 0.0)
        grad_updates = dot3(cut(mix), grad_parts, "tn")
        solved = [None] * blocks
        for block in reversed(range(blocks)):
            span = slice(block * SUB, (block + 1) * SUB)
            rest = grad_updates[span]
            for after in range(block + 1, blocks):
                later = slice(after * SUB, (after + 1) * SUB)
                rest = rest - dot3(cut(coupling[later, span]), cut(solved[after]), "tn")
            solved[block] = dot3(cut(inverse_ref[local, block]), cut(rest), "tn")
        grad_target = jnp.concatenate(solved, 0)
        grad_coupling = jnp.where(strict, -dot3(cut(grad_target), updates, "nt"), 0.0)
        grad_value = beta * grad_target
        grad_beta = jnp.sum(grad_target * value, -1, keepdims=True) + jnp.sum(
            grad_coupling * pair, -1, keepdims=True
        )
        flow = cut(grad_coupling * coupling + grad_mix * mix)
        run = dot1(upper, flow[0]) + dot1(upper, flow[1])
        grad_log = jnp.sum(jnp.where(strict, run, 0.0), -1, keepdims=True)
        grad_pair = cut(grad_coupling * beta * decay)
        grad_cross = cut(grad_mix * decay)
        grad_query = dot3(grad_cross, key_parts)
        grad_key = (
            dot3(grad_cross, query_parts, "tn")
            + dot3(grad_pair, key_parts)
            + dot3(grad_pair, key_parts, "tn")
        )
        grad_query_raw, grad_conv = conv_back(
            unit_back(grad_query, query_conv, query_sigma, query_act, query_inv, scale),
            query_raw, conv_query_ref[:, kcut],
        )
        conv_query_out[:, kcut] = grad_conv
        grad_key_raw, grad_conv = conv_back(
            unit_back(grad_key, key_conv, key_sigma, key_act, key_inv, 1.0),
            key_raw, conv_key_ref[:, kcut],
        )
        conv_key_out[:, kcut] = grad_conv
        grad_value_raw, grad_conv = conv_back(
            grad_value * silu_slope(value_conv, value_sigma), value_raw, conv_value_ref[:, vcut]
        )
        conv_value_out[:, vcut] = grad_conv
        key_start = pl.multiple_of(head * key_dim, key_dim)
        value_start = pl.multiple_of(head * value_dim, value_dim)
        grads_ref[:, pl.ds(offsets[0] + key_start, key_dim)] = grad_query_raw.astype(bf16)
        grads_ref[:, pl.ds(offsets[1] + key_start, key_dim)] = grad_key_raw.astype(bf16)
        grads_ref[:, pl.ds(offsets[2] + value_start, value_dim)] = grad_value_raw.astype(bf16)
        grads_ref[:, pl.ds(offsets[3] + value_start, value_dim)] = grad_gate.astype(bf16)
        beta_acc[...] += jnp.where(lane == head, grad_beta, 0.0)
        gate_acc[...] += jnp.where(lane == heads + head, grad_log, 0.0)

    @pl.when(step == pl.num_programs(0) - 1)
    def _():
        grad_log = gate_acc[...]
        grad_decay = grad_log * slope_all
        grad_small = beta_acc[...] * beta_all * (1.0 - beta_all) + grad_decay
        grads_ref[:, offsets[4] : offsets[4] + 2 * heads] = grad_small.astype(bf16)
        lanes_out[0:1, :] = jnp.sum(grad_log * gates_all, 0, keepdims=True)
        lanes_out[1:2, :] = jnp.sum(grad_decay, 0, keepdims=True)


def mixer_layout(projections, heads, key_cols, value_cols, per_step):
    length = projections.shape[0]
    key_dim = key_cols // heads
    value_dim = value_cols // heads
    wide_key = per_step * key_dim
    wide_value = per_step * value_dim
    taps_of = lambda taps: [
        pl.BlockSpec((taps, wide_key), lambda g: (0, g)),
        pl.BlockSpec((taps, wide_key), lambda g: (0, g)),
        pl.BlockSpec((taps, wide_value), lambda g: (0, g)),
    ]
    key_at = key_cols // wide_key
    value_at = 2 * key_cols // wide_value
    gate_at = (2 * key_cols + value_cols) // wide_value
    columns = [
        pl.BlockSpec((length, wide_key), lambda g: (0, g)),
        pl.BlockSpec((length, wide_key), lambda g: (0, key_at + g)),
        pl.BlockSpec((length, wide_value), lambda g: (0, value_at + g)),
        pl.BlockSpec((length, wide_value), lambda g: (0, gate_at + g)),
        pl.BlockSpec((length, 2 * heads), lambda g: (0, 0)),
        pl.BlockSpec((2, 2 * heads), lambda g: (0, 0)),
    ]
    rows = pl.BlockSpec((length, wide_value), lambda g: (0, g))
    blocks = length // SUB
    inverse = pl.BlockSpec((per_step, blocks, SUB, SUB), lambda g: (g, 0, 0, 0))
    gain = pl.BlockSpec((1, value_dim), lambda g: (0, 0))
    return columns, taps_of, rows, inverse, gain, key_dim, value_dim


def mixer_forward(projections, small, lanes, convs, gain, heads, key_cols, value_cols, per_step=2):
    length = projections.shape[0]
    taps = convs[0].shape[0]
    columns, taps_of, rows, inverse, gain_spec, key_dim, value_dim = mixer_layout(
        projections, heads, key_cols, value_cols, per_step
    )
    return pl.pallas_call(
        functools.partial(forward_kernel, heads, per_step, key_dim, value_dim),
        grid=(heads // per_step,),
        in_specs=columns + taps_of(taps) + [gain_spec],
        out_specs=[rows, rows, rows, inverse],
        out_shape=[
            jax.ShapeDtypeStruct((length, value_cols), bf16),
            jax.ShapeDtypeStruct((length, value_cols), f32),
            jax.ShapeDtypeStruct((length, value_cols), f32),
            jax.ShapeDtypeStruct((heads, length // SUB, SUB, SUB), f32),
        ],
        name="mixer_forward",
    )(projections, projections, projections, projections, small, lanes, *convs, gain)


def mixer_backward(
    projections, small, lanes, convs, gain, mixed, updates, inverses, grad_mixed,
    heads, key_cols, value_cols, per_step=2,
):
    length, width = projections.shape
    taps = convs[0].shape[0]
    columns, taps_of, rows, inverse, gain_spec, key_dim, value_dim = mixer_layout(
        projections, heads, key_cols, value_cols, per_step
    )
    offsets = (
        0, key_cols, 2 * key_cols, 2 * key_cols + value_cols, 2 * key_cols + 2 * value_cols
    )
    return pl.pallas_call(
        functools.partial(backward_kernel, heads, per_step, key_dim, value_dim, offsets),
        grid=(heads // per_step,),
        in_specs=columns + taps_of(taps) + [gain_spec, rows, rows, inverse, rows],
        out_specs=[pl.BlockSpec((length, width), lambda g: (0, 0))]
        + taps_of(taps)
        + [
            pl.BlockSpec((1, value_dim), lambda g: (0, 0)),
            pl.BlockSpec((2, 2 * heads), lambda g: (0, 0)),
        ],
        out_shape=[
            jax.ShapeDtypeStruct((length, width), bf16),
            jax.ShapeDtypeStruct((taps, key_cols), f32),
            jax.ShapeDtypeStruct((taps, key_cols), f32),
            jax.ShapeDtypeStruct((taps, value_cols), f32),
            jax.ShapeDtypeStruct((1, value_dim), f32),
            jax.ShapeDtypeStruct((2, 2 * heads), f32),
        ],
        scratch_shapes=[
            pltpu.VMEM((length, 2 * heads), f32),
            pltpu.VMEM((length, 2 * heads), f32),
        ],
        name="mixer_backward",
    )(
        projections, projections, projections, projections, small, lanes, *convs, gain,
        mixed, updates, inverses, grad_mixed,
    )


def plain_dot(left, right):
    return jnp.dot(left, right, preferred_element_type=f32)


def left_dot(left, right):
    return lax.dot_general(left, right, dims_of("tn"), preferred_element_type=f32)


def right_dot(left, right):
    return lax.dot_general(left, right, dims_of("nt"), preferred_element_type=f32)


def rms_rows(inputs, gain):
    wide_rows = inputs.astype(f32)
    inverse = lax.rsqrt(jnp.mean(wide_rows * wide_rows, -1, keepdims=True) + 1e-05)
    normed = wide_rows * inverse
    return (normed, inverse, (normed * gain).astype(bf16))


def rms_back(grad_rows, normed, inverse, gain):
    scaled = grad_rows * gain
    grad_in = inverse * (scaled - normed * jnp.mean(scaled * normed, -1, keepdims=True))
    return (grad_in, jnp.sum(grad_rows * normed, 0))


class Ring:
    def __init__(self, axis):
        self.axis = axis
        self.chips = lax.axis_size(axis) // 2
        evens = [chip for chip in range(self.chips) if chip % 2 == 0]
        odds = [chip for chip in range(self.chips) if chip % 2 == 1]
        order = evens + odds[::-1]
        following = [(order[i], order[(i + 1) % self.chips]) for i in range(self.chips)]
        self.ahead = [(2 * a + c, 2 * b + c) for a, b in following for c in (0, 1)]
        self.behind = [(2 * b + c, 2 * a + c) for a, b in following for c in (0, 1)]
        self.pairs = [(i, i ^ 1) for i in range(2 * self.chips)]
        index = lax.axis_index(axis)
        self.core = index % 2
        chip = index // 2
        self.position = jnp.where(
            chip % 2 == 0, chip // 2, self.chips - 1 - (chip - 1) // 2
        )

    def chip_at(self, shift):
        spot = (self.position + shift) % self.chips
        evens = (self.chips + 1) // 2
        return jnp.where(spot < evens, 2 * spot, 2 * (self.chips - 1 - spot) + 1)

    def forward(self, array):
        return lax.ppermute(array, self.axis, self.ahead)

    def backward(self, array):
        return lax.ppermute(array, self.axis, self.behind)

    def partner(self, array):
        return lax.ppermute(array, self.axis, self.pairs)

    def gather(self, shard):
        if self.chips > UNROLLED_CHIPS:
            return lax.all_gather(shard, self.axis, axis=0, tiled=True), shard
        rows = shard.shape[0]
        full = jnp.zeros((2 * self.chips * rows, shard.shape[1]), shard.dtype)

        def place(full, piece, shift, skip=0):
            base = 2 * self.chip_at(shift) * rows + skip
            full = lax.dynamic_update_slice(full, piece, (base + self.core * rows, 0))
            return lax.dynamic_update_slice(
                full, self.partner(piece), (base + (1 - self.core) * rows, 0)
            )

        full = place(full, shard, 0)
        ahead = behind = shard
        half = self.chips // 2
        for step in range(1, half):
            ahead = self.forward(ahead)
            behind = self.backward(behind)
            full = place(full, ahead, -step)
            full = place(full, behind, step)
        late = (ahead, behind)
        cut_row = rows // 2
        full = place(full, self.forward(ahead[:cut_row]), -half)
        full = place(full, self.backward(behind[cut_row:]), half, cut_row)
        return full, late

    def scatter(self, partial):
        if self.chips > UNROLLED_CHIPS:
            return lax.psum_scatter(
                partial.astype(f32), self.axis, scatter_dimension=0, tiled=True
            )
        rows = partial.shape[0] // (2 * self.chips)
        cut_row = rows // 2
        half = self.chips // 2

        def chunk(shift, core):
            start = (2 * self.chip_at(shift) + core) * rows
            return lax.dynamic_slice_in_dim(partial, start, rows, 0)

        def both(shift):
            mine = chunk(shift, self.core).astype(f32)
            return mine + self.partner(chunk(shift, 1 - self.core)).astype(f32)

        far = both(half).astype(bf16)
        ahead = self.forward(far[:cut_row])
        behind = self.backward(far[cut_row:])
        ahead_rows = slice(0, cut_row)
        behind_rows = slice(cut_row, rows)
        for step in range(half - 1, 0, -1):
            own = both(step)
            if step == half - 1:
                own = jnp.concatenate([own[:cut_row] + ahead.astype(f32), own[cut_row:]], 0)
            else:
                own = own + ahead.astype(f32)
            mirrored = both(-step)
            if step == half - 1:
                mirrored = jnp.concatenate(
                    [mirrored[:cut_row], mirrored[cut_row:] + behind.astype(f32)], 0
                )
            else:
                mirrored = mirrored + behind.astype(f32)
            ahead = self.forward(own.astype(bf16))
            behind = self.backward(mirrored.astype(bf16))
        own = both(0)
        if half == 1:
            return own + jnp.concatenate([ahead, behind], 0).astype(f32)
        return own + ahead.astype(f32) + behind.astype(f32)

    def total(self, array):
        size = 1
        while size < 2 * self.chips:
            flips = [(i, i ^ size) for i in range(2 * self.chips)]
            array = array + lax.ppermute(array, self.axis, flips)
            size = 2 * size
        return array


def others_of(array, axis):
    count = lax.axis_size(axis)
    received = []
    for shift in range(1, count):
        moves = [(i, (i + shift) % count) for i in range(count)]
        received.append(lax.ppermute(array, axis, moves))
    return received


def by_index(axis, pieces, dim):
    count = lax.axis_size(axis)
    index = lax.axis_index(axis)
    joined = None
    for value in range(count):
        here = jnp.concatenate([pieces[(value - i) % count] for i in range(count)], dim)
        joined = here if joined is None else jnp.where(index == value, here, joined)
    return joined


def gather_rows(array, axis):
    return by_index(axis, [array] + others_of(array, axis), 0)


def scatter_rows(partial, axis):
    count = lax.axis_size(axis)
    index = lax.axis_index(axis)
    rows = partial.shape[0] // count
    total = lax.dynamic_slice_in_dim(partial, index * rows, rows, 0)
    for shift in range(1, count):
        target = (index + shift) % count
        part = lax.dynamic_slice_in_dim(partial, target * rows, rows, 0).astype(bf16)
        moves = [(i, (i + shift) % count) for i in range(count)]
        total = total + lax.ppermute(part, axis, moves).astype(f32)
    return total


def after(array, done):
    return lax.optimization_barrier((array, done))[0]


def split_columns(array, widths):
    pieces = []
    offset = 0
    for width in widths:
        pieces.append(array[:, offset : offset + width])
        offset = offset + width
    return pieces


def on_device(
    tokens, out_cotangent, seq_lengths, norm_gain1, query_weight, key_weight, value_weight,
    out_gate_weight, beta_weight, decay_weight, conv_query, conv_key, conv_value,
    decay_log_rate, decay_bias, out_gain, out_weight, norm_gain2, ffn_gate_weight,
    ffn_up_weight, ffn_down_weight,
):
    ring = Ring("dp")
    local_rows = tokens.shape[0]
    tensor_index = lax.axis_index("tensor")
    tensor_count = lax.axis_size("tensor")
    seq_length = seq_lengths[0]
    local_pos = tensor_index * local_rows + jnp.arange(local_rows, dtype=jnp.int32)
    local_mask = (local_pos < seq_length).astype(f32)[:, None]
    key_cols = query_weight.shape[1]
    value_cols = value_weight.shape[1]
    heads = beta_weight.shape[1]
    hidden_cols = ffn_gate_weight.shape[1]
    mixer_widths = [key_cols, key_cols, value_cols, value_cols, heads, heads]
    small_at = 2 * key_cols + 2 * value_cols
    mixer_joined = jnp.concatenate(
        [query_weight, key_weight, value_weight, out_gate_weight, beta_weight, decay_weight], axis=1
    )
    ffn_joined = jnp.concatenate([ffn_gate_weight, ffn_up_weight], axis=1)
    mixer_full, late = ring.gather(mixer_joined)
    out_full, late = ring.gather(after(out_weight, late))
    ffn_full, late = ring.gather(after(ffn_joined, late))
    down_full, late = ring.gather(after(ffn_down_weight, late))

    normed1, inverse1, hidden1 = rms_rows(tokens, norm_gain1)
    whole1 = gather_rows(hidden1, "tensor")
    grad_local = (local_mask * out_cotangent.astype(f32)).astype(bf16)
    grad_whole = gather_rows(grad_local, "tensor")
    projections = plain_dot(whole1, mixer_full)
    small = projections[:, small_at:]
    blank = jnp.zeros((heads,), f32)
    lanes = jnp.stack(
        [jnp.concatenate([blank, decay_log_rate]), jnp.concatenate([blank, decay_bias])]
    )
    convs = (conv_query, conv_key, conv_value)
    gain_row = out_gain[None]
    mixed_half, mixed, updates, inverses = mixer_forward(
        projections, small, lanes, convs, gain_row, heads, key_cols, value_cols
    )
    branch = scatter_rows(right_dot(mixed_half, out_full), "tensor")
    residual = tokens.astype(f32) + branch
    normed2, inverse2, hidden2 = rms_rows(residual, norm_gain2)
    whole2 = gather_rows(hidden2, "tensor")
    pre_both = plain_dot(whole2, ffn_full)
    gate_pre = pre_both[:, :hidden_cols]
    up_pre = pre_both[:, hidden_cols:]
    sigma_gate = jax.nn.sigmoid(gate_pre)
    gate_act = gate_pre * sigma_gate
    inner_act = (gate_act * up_pre).astype(bf16)
    grad_inner = plain_dot(grad_whole, down_full)
    grad_gate_pre = (
        grad_inner * up_pre * sigma_gate * (1.0 + gate_pre * (1.0 - sigma_gate))
    ).astype(bf16)
    grad_up_pre = (grad_inner * gate_act).astype(bf16)
    grad_pre_both = jnp.concatenate([grad_gate_pre, grad_up_pre], axis=1)
    grad_hidden2 = scatter_rows(right_dot(grad_pre_both, ffn_full), "tensor")
    down_shard = ring.scatter(left_dot(grad_whole, inner_act).astype(bf16))
    ffn_shard = ring.scatter(left_dot(whole2, grad_pre_both).astype(bf16))
    ffn_branch = scatter_rows(right_dot(inner_act, down_full), "tensor")
    output = (local_mask * (residual + ffn_branch)).astype(bf16)
    grad_normed2, second_gain_gradient = rms_back(grad_hidden2, normed2, inverse2, norm_gain2)
    grad_residual = local_mask * out_cotangent.astype(f32) + grad_normed2
    grad_whole1 = gather_rows(grad_residual.astype(bf16), "tensor")
    grad_mixed = plain_dot(grad_whole1, out_full)
    out_shard = ring.scatter(left_dot(grad_whole1, mixed_half).astype(bf16))
    grad_projs, grad_conv_query, grad_conv_key, grad_conv_value, gain_sum, lane_sums = mixer_backward(
        projections, small, lanes, convs, gain_row, mixed, updates, inverses, grad_mixed,
        heads, key_cols, value_cols,
    )
    proj_shard = ring.scatter(left_dot(whole1, grad_projs).astype(bf16))
    grad_hidden1 = scatter_rows(right_dot(grad_projs, mixer_full), "tensor")
    grad_normed1, first_gain_gradient = rms_back(grad_hidden1, normed1, inverse1, norm_gain1)
    grad_tokens = (grad_residual + grad_normed1).astype(bf16)
    mixer_grads = split_columns(proj_shard, mixer_widths)
    ffn_grads = split_columns(ffn_shard, [hidden_cols, hidden_cols])

    taps = conv_query.shape[0]
    key_end = taps * key_cols
    value_end = taps * value_cols
    flat = [
        grad_conv_query.reshape(-1),
        grad_conv_key.reshape(-1),
        grad_conv_value.reshape(-1),
        lane_sums.reshape(-1),
    ]
    own_size = sum(member.shape[0] for member in flat)
    shared = [first_gain_gradient, second_gain_gradient, gain_sum.reshape(-1)]
    flat = jnp.concatenate(flat + shared)
    size = flat.shape[0]
    lanes_wide = 1024
    padded = -(-size // lanes_wide) * lanes_wide
    packed = jnp.pad(flat, (0, padded - size)).reshape(-1, lanes_wide)
    packed = ring.total(packed)
    pieces = [member.reshape(-1) for member in [packed] + others_of(packed, "tensor")]
    summed = pieces[0]
    for member in pieces[1:]:
        summed = summed + member

    def joined(start, rows, cols):
        parts = [member[start : start + rows * cols].reshape(rows, cols) for member in pieces]
        return by_index("tensor", parts, 1)

    lanes_at = 2 * key_end + value_end
    rates = joined(lanes_at + heads, 1, heads)[0]
    biases = joined(lanes_at + 3 * heads, 1, heads)[0]
    width1 = norm_gain1.shape[0]
    width2 = norm_gain2.shape[0]
    gain1_at = own_size
    gain2_at = own_size + width1
    gain_at = gain2_at + width2
    return (
        output,
        grad_tokens,
        summed[gain1_at : gain1_at + width1],
        mixer_grads[0],
        mixer_grads[1],
        mixer_grads[2],
        mixer_grads[3],
        mixer_grads[4],
        mixer_grads[5],
        joined(0, taps, key_cols),
        joined(key_end, taps, key_cols),
        joined(2 * key_end, taps, value_cols),
        rates,
        biases,
        summed[gain_at : gain_at + out_gain.shape[0]],
        out_shard,
        summed[gain2_at : gain2_at + width2],
        ffn_grads[0],
        ffn_grads[1],
        down_shard,
    )


def solution(mesh):
    in_specs = (
        P(("dp", "tensor"), None),
        P(("dp", "tensor"), None),
        P("dp"),
        P(),
        P("dp", "tensor"),
        P("dp", "tensor"),
        P("dp", "tensor"),
        P("dp", "tensor"),
        P("dp", "tensor"),
        P("dp", "tensor"),
        P(None, "tensor"),
        P(None, "tensor"),
        P(None, "tensor"),
        P("tensor"),
        P("tensor"),
        P(),
        P("dp", "tensor"),
        P(),
        P("dp", "tensor"),
        P("dp", "tensor"),
        P("dp", "tensor"),
    )
    out_specs = (
        P(("dp", "tensor"), None),
        P(("dp", "tensor"), None),
        P(),
        P("dp", "tensor"),
        P("dp", "tensor"),
        P("dp", "tensor"),
        P("dp", "tensor"),
        P("dp", "tensor"),
        P("dp", "tensor"),
        P(),
        P(),
        P(),
        P(),
        P(),
        P(),
        P("dp", "tensor"),
        P(),
        P("dp", "tensor"),
        P("dp", "tensor"),
        P("dp", "tensor"),
    )
    return jax.shard_map(
        on_device, mesh=mesh, in_specs=in_specs, out_specs=out_specs, check_vma=False
    )
```

```python
import functools

import jax
import jax.numpy as jnp
from jax import lax
from jax.experimental import pallas as pl
from jax.experimental.pallas import tpu as pltpu
from jax.sharding import PartitionSpec as P


SUB = 128
LANES = 128
UNROLLED_CHIPS = 16
bf16 = jnp.bfloat16
f32 = jnp.float32


def dims_of(kind):
    return {
        "nn": (((1,), (0,)), ((), ())),
        "nt": (((1,), (1,)), ((), ())),
        "tn": (((0,), (0,)), ((), ())),
    }[kind]


def dot1(left, right, kind="nn"):
    return lax.dot_general(left, right, dims_of(kind), preferred_element_type=f32)


def cut(array):
    high = array.astype(bf16)
    return (high, (array - high.astype(f32)).astype(bf16))


def dot3(left, right, kind="nn"):
    return (
        dot1(left[0], right[0], kind)
        + dot1(left[0], right[1], kind)
        + dot1(left[1], right[0], kind)
    )


def shift_down(array, amount):
    if amount == 0:
        return array
    rows = lax.broadcasted_iota(jnp.int32, array.shape, 0)
    return jnp.where(rows >= amount, pltpu.roll(array, amount, 0), 0.0)


def shift_up(array, amount):
    if amount == 0:
        return array
    length = array.shape[0]
    rows = lax.broadcasted_iota(jnp.int32, array.shape, 0)
    return jnp.where(rows < length - amount, pltpu.roll(array, length - amount, 0), 0.0)


def conv_rows(projected, kernel):
    taps = kernel.shape[0]
    summed = kernel[taps - 1 : taps] * projected
    for offset in range(1, taps):
        tap = taps - 1 - offset
        summed = summed + kernel[tap : tap + 1] * shift_down(projected, offset)
    return summed


def conv_back(grad_conv, projected, kernel):
    taps = kernel.shape[0]
    grad_proj = kernel[taps - 1 : taps] * grad_conv
    for offset in range(1, taps):
        tap = taps - 1 - offset
        grad_proj = grad_proj + kernel[tap : tap + 1] * shift_up(grad_conv, offset)
    terms = []
    for tap in range(taps):
        moved = shift_down(projected, taps - 1 - tap)
        terms.append(jnp.sum(grad_conv * moved, 0, keepdims=True))
    return grad_proj, jnp.concatenate(terms, 0)


def silu_slope(values, sigma):
    return sigma * (1.0 + values * (1.0 - sigma))


def gate_rows(small, lanes_ref, heads):
    lane = lax.broadcasted_iota(jnp.int32, small.shape, 1)
    rate = jnp.exp(lanes_ref[0:1, :])
    shifted = small + lanes_ref[1:2, :]
    soft = jnp.maximum(shifted, 0.0) + jnp.log1p(jnp.exp(-jnp.abs(shifted)))
    gates = jnp.where(lane >= heads, -rate * soft, 0.0)
    slope = jnp.where(lane >= heads, -rate * jax.nn.sigmoid(shifted), 0.0)
    return jax.nn.sigmoid(small), gates, slope


def sum_gates(gates):
    length = gates.shape[0]
    row = lax.broadcasted_iota(jnp.int32, (length, length), 0)
    col = lax.broadcasted_iota(jnp.int32, (length, length), 1)
    lower = (row >= col).astype(f32)
    upper = (row <= col).astype(f32)
    kwargs = dict(precision=lax.Precision.HIGHEST, preferred_element_type=f32)
    by_row = lax.dot_general(lower, gates, dims_of("nn"), **kwargs)
    by_col = lax.dot_general(gates, upper, dims_of("tn"), **kwargs)
    return by_row, by_col


def lane_pick(array, index):
    lane = lax.broadcasted_iota(jnp.int32, array.shape, 1)
    return jnp.sum(jnp.where(lane == index, array, 0.0), 1, keepdims=True)


def row_pick(array, index):
    row = lax.broadcasted_iota(jnp.int32, array.shape, 0)
    return jnp.sum(jnp.where(row == index, array, 0.0), 0, keepdims=True)


def decay_square(cum_col, cum_row):
    length = cum_col.shape[0]
    row = lax.broadcasted_iota(jnp.int32, (length, length), 0)
    col = lax.broadcasted_iota(jnp.int32, (length, length), 1)
    keep = row >= col
    square = jnp.where(keep, jnp.exp(jnp.where(keep, cum_col - cum_row, 0.0)), 0.0)
    return square, keep, row > col


def unit_rows(raw, kernel):
    conv = conv_rows(raw, kernel)
    sigma = jax.nn.sigmoid(conv)
    act = conv * sigma
    inverse = lax.rsqrt(jnp.sum(act * act, -1, keepdims=True) + 1e-06)
    return conv, sigma, act, inverse


def fetch(pieces, starts_ref, target, sems, cols):
    copies = []
    for i, piece in enumerate(pieces):
        rows = piece.shape[0]
        start = pl.multiple_of(starts_ref[i], rows)
        copies.append(
            pltpu.make_async_copy(
                piece.at[:, cols], target.at[pl.ds(start, rows), :], sems.at[i]
            )
        )
    for copy in copies:
        copy.start()
    return copies


def spill(chunks, starts_ref, source, sems):
    copies = []
    for i, chunk in enumerate(chunks):
        rows = chunk.shape[0]
        start = pl.multiple_of(starts_ref[i], rows)
        copies.append(pltpu.make_async_copy(source.at[pl.ds(start, rows), :], chunk, sems.at[i]))
    for copy in copies:
        copy.start()
    return copies


def wait_all(copies):
    for copy in copies:
        copy.wait()


def outer(left_ref, right, target_ref):
    total = left_ref.shape[1]
    step = 256 if total % 256 == 0 else total
    for start in range(0, total, step):
        span = slice(start, start + step)
        target_ref[span, :] = dot1(left_ref[:, span], right, "tn").astype(bf16)


def head_cuts(local, per_step, key_dim, value_dim):
    wide_key = per_step * key_dim
    wide_value = per_step * value_dim
    kcut = slice(local * key_dim, (local + 1) * key_dim)
    vcut = slice(local * value_dim, (local + 1) * value_dim)
    starts = (
        local * key_dim,
        wide_key + local * key_dim,
        2 * wide_key + local * value_dim,
        2 * wide_key + wide_value + local * value_dim,
    )
    widths = (key_dim, key_dim, value_dim, value_dim)
    pieces = [slice(start, start + width) for start, width in zip(starts, widths)]
    return kcut, vcut, pieces


def forward_kernel(
    heads, group, per_step, key_dim, value_dim, count,
    starts_ref, x_ref, lanes_ref, conv_query_ref, conv_key_ref, conv_value_ref, gain_ref, *refs
):
    pieces = refs[:count]
    proj_ref, small_ref, half_ref, mixed_ref, update_ref, inverse_ref = refs[count : count + 6]
    weight_ref, small_weight_ref, sems = refs[count + 6 :]
    width = proj_ref.shape[1]
    end = pieces[0].shape[1]
    copies = fetch(
        pieces, starts_ref, weight_ref, sems.at[0], slice(group * width, (group + 1) * width)
    )
    copies += fetch(pieces, starts_ref, small_weight_ref, sems.at[1], slice(end - LANES, end))
    wait_all(copies)
    small_ref[...] = dot1(x_ref[...], small_weight_ref[...])
    proj_ref[...] = dot1(x_ref[...], weight_ref[...])
    length = proj_ref.shape[0]
    blocks = length // SUB
    beta_all, gates_all, _ = gate_rows(small_ref[...], lanes_ref, heads)
    cum_all, cum_rows = sum_gates(gates_all)
    sub_row = lax.broadcasted_iota(jnp.int32, (SUB, SUB), 0)
    sub_col = lax.broadcasted_iota(jnp.int32, (SUB, SUB), 1)
    state = []
    for local in range(per_step):
        head = group * per_step + local
        kcut, vcut, pieces = head_cuts(local, per_step, key_dim, value_dim)
        _, _, query_act, query_inv = unit_rows(proj_ref[:, pieces[0]], conv_query_ref[:, kcut])
        query = query_act * query_inv * key_dim ** (-0.5)
        _, _, key_act, key_inv = unit_rows(proj_ref[:, pieces[1]], conv_key_ref[:, kcut])
        key = key_act * key_inv
        value_conv = conv_rows(proj_ref[:, pieces[2]], conv_value_ref[:, vcut])
        value = value_conv * jax.nn.sigmoid(value_conv)
        beta = lane_pick(beta_all, head)
        decay, _, strict = decay_square(
            lane_pick(cum_all, heads + head), row_pick(cum_rows, heads + head)
        )
        key_parts = cut(key)
        coupling = jnp.where(strict, beta * dot3(key_parts, key_parts, "nt") * decay, 0.0)
        mix = dot3(cut(query), key_parts, "nt") * decay
        state.append((coupling, mix, beta * value))
    inverses = []
    for coupling, _, _ in state:
        parts = []
        for block in range(blocks):
            span = slice(block * SUB, (block + 1) * SUB)
            parts.append(coupling[span, span])
        inverses.append(parts)
    squares = [[part for part in parts] for parts in inverses]
    eye = (sub_row == sub_col).astype(f32)
    size = 1
    current = [[None] * blocks for _ in state]
    while size < SUB:
        member = ((sub_row // (2 * size)) == (sub_col // (2 * size))) & (
            (sub_row // size) != (sub_col // size)
        )
        for h in range(per_step):
            for block in range(blocks):
                cross = jnp.where(member, squares[h][block], 0.0)
                if size == 1:
                    current[h][block] = eye - cross
                else:
                    now = cut(current[h][block])
                    inner = dot3(cut(cross), now)
                    current[h][block] = current[h][block] - dot3(now, cut(inner))
        size = 2 * size
    for local in range(per_step):
        _, vcut, pieces = head_cuts(local, per_step, key_dim, value_dim)
        coupling, mix, target = state[local]
        solved = []
        for block in range(blocks):
            span = slice(block * SUB, (block + 1) * SUB)
            rest = target[span]
            for before in range(block):
                past = slice(before * SUB, (before + 1) * SUB)
                rest = rest - dot3(cut(coupling[span, past]), cut(solved[before]))
            solved.append(dot3(cut(current[local][block]), cut(rest)))
            inverse_ref[local, block] = current[local][block]
        updates = jnp.concatenate(solved, 0)
        mixed = dot3(cut(mix), cut(updates))
        update_ref[:, vcut] = updates
        mixed_ref[:, vcut] = mixed
        inverse = lax.rsqrt(jnp.mean(mixed * mixed, -1, keepdims=True) + 1e-05)
        gate = proj_ref[:, pieces[3]]
        half_ref[:, vcut] = (
            mixed * inverse * gain_ref[...] * (gate * jax.nn.sigmoid(gate))
        ).astype(bf16)


def unit_back(grad, conv, sigma, act, inverse, scale):
    inner = jnp.sum(grad * act, -1, keepdims=True)
    grad_act = scale * inverse * (grad - act * (inverse * inverse) * inner)
    return grad_act * silu_slope(conv, sigma)


def backward_kernel(
    heads, group, per_step, key_dim, value_dim, last, count, out_count,
    starts_ref, x_ref, grad_rows_ref, proj_ref, small_ref, lanes_ref,
    conv_query_ref, conv_key_ref, conv_value_ref, gain_ref,
    mixed_ref, update_ref, inverse_ref, carry_ref, hidden_ref, *refs
):
    pieces = refs[:count]
    out_pieces = refs[count : count + out_count]
    refs = refs[count + out_count :]
    chunks = refs[:count]
    conv_query_out, conv_key_out, conv_value_out, gain_out, carry_out, lanes_out, hidden_out = refs[
        count : count + 7
    ]
    weight_ref, out_weight_ref, grads_ref, sum_ref, sems = refs[count + 7 :]
    width = grads_ref.shape[1]
    value_width = mixed_ref.shape[1]
    grouped = 2 * per_step * (key_dim + value_dim)
    out_copies = fetch(
        out_pieces, starts_ref, out_weight_ref, sems.at[0],
        slice(group * value_width, (group + 1) * value_width),
    )
    copies = fetch(
        pieces, starts_ref, weight_ref, sems.at[1], slice(group * grouped, group * grouped + width)
    )
    wait_all(out_copies)
    grad_all = dot1(grad_rows_ref[...], out_weight_ref[...])
    length = proj_ref.shape[0]
    blocks = length // SUB
    small = small_ref[...]
    beta_all, gates_all, slope_all = gate_rows(small, lanes_ref, heads)
    cum_all, cum_rows = sum_gates(gates_all)
    lane = lax.broadcasted_iota(jnp.int32, small.shape, 1)
    upper = (
        lax.broadcasted_iota(jnp.int32, (length, length), 0)
        <= lax.broadcasted_iota(jnp.int32, (length, length), 1)
    ).astype(bf16)

    carry = carry_ref[...]
    gain_sum = jnp.zeros((1, value_dim), f32)
    for local in range(per_step):
        head = group * per_step + local
        kcut, vcut, pieces = head_cuts(local, per_step, key_dim, value_dim)
        scale = key_dim ** (-0.5)
        query_raw = proj_ref[:, pieces[0]]
        key_raw = proj_ref[:, pieces[1]]
        value_raw = proj_ref[:, pieces[2]]
        query_conv, query_sigma, query_act, query_inv = unit_rows(
            query_raw, conv_query_ref[:, kcut]
        )
        query = query_act * query_inv * scale
        key_conv, key_sigma, key_act, key_inv = unit_rows(key_raw, conv_key_ref[:, kcut])
        key = key_act * key_inv
        value_conv = conv_rows(value_raw, conv_value_ref[:, vcut])
        value_sigma = jax.nn.sigmoid(value_conv)
        value = value_conv * value_sigma
        mixed = mixed_ref[:, vcut]
        inverse = lax.rsqrt(jnp.mean(mixed * mixed, -1, keepdims=True) + 1e-05)
        gate = proj_ref[:, pieces[3]]
        gate_sigma = jax.nn.sigmoid(gate)
        gain = gain_ref[...]
        normed = mixed * inverse
        grad_out = grad_all[:, vcut]
        through = grad_out * normed
        grad_gate = through * gain * silu_slope(gate, gate_sigma)
        swish = gate * gate_sigma
        gain_sum = gain_sum + jnp.sum(through * swish, 0, keepdims=True)
        grad_normed = grad_out * gain * swish
        grad_mixed = inverse * (
            grad_normed - normed * jnp.mean(grad_normed * normed, -1, keepdims=True)
        )
        beta = lane_pick(beta_all, head)
        decay, keep, strict = decay_square(
            lane_pick(cum_all, heads + head), row_pick(cum_rows, heads + head)
        )
        key_parts = cut(key)
        query_parts = cut(query)
        pair = dot3(key_parts, key_parts, "nt") * decay
        coupling = jnp.where(strict, beta * pair, 0.0)
        mix = dot3(query_parts, key_parts, "nt") * decay
        updates = cut(update_ref[:, vcut])
        grad_parts = cut(grad_mixed)
        grad_mix = jnp.where(keep, dot3(grad_parts, updates, "nt"), 0.0)
        grad_updates = dot3(cut(mix), grad_parts, "tn")
        solved = [None] * blocks
        for block in reversed(range(blocks)):
            span = slice(block * SUB, (block + 1) * SUB)
            rest = grad_updates[span]
            for after in range(block + 1, blocks):
                later = slice(after * SUB, (after + 1) * SUB)
                rest = rest - dot3(cut(coupling[later, span]), cut(solved[after]), "tn")
            solved[block] = dot3(cut(inverse_ref[local, block]), cut(rest), "tn")
        grad_target = jnp.concatenate(solved, 0)
        grad_coupling = jnp.where(strict, -dot3(cut(grad_target), updates, "nt"), 0.0)
        grad_value = beta * grad_target
        grad_beta = jnp.sum(grad_target * value, -1, keepdims=True) + jnp.sum(
            grad_coupling * pair, -1, keepdims=True
        )
        flow = cut(grad_coupling * coupling + grad_mix * mix)
        run = dot1(upper, flow[0]) + dot1(upper, flow[1])
        grad_log = jnp.sum(jnp.where(strict, run, 0.0), -1, keepdims=True)
        grad_pair = cut(grad_coupling * beta * decay)
        grad_cross = cut(grad_mix * decay)
        grad_query = dot3(grad_cross, key_parts)
        grad_key = (
            dot3(grad_cross, query_parts, "tn")
            + dot3(grad_pair, key_parts)
            + dot3(grad_pair, key_parts, "tn")
        )
        grad_query_raw, grad_conv = conv_back(
            unit_back(grad_query, query_conv, query_sigma, query_act, query_inv, scale),
            query_raw, conv_query_ref[:, kcut],
        )
        conv_query_out[:, kcut] = grad_conv
        grad_key_raw, grad_conv = conv_back(
            unit_back(grad_key, key_conv, key_sigma, key_act, key_inv, 1.0),
            key_raw, conv_key_ref[:, kcut],
        )
        conv_key_out[:, kcut] = grad_conv
        grad_value_raw, grad_conv = conv_back(
            grad_value * silu_slope(value_conv, value_sigma), value_raw, conv_value_ref[:, vcut]
        )
        conv_value_out[:, vcut] = grad_conv
        grads_ref[:, pieces[0]] = grad_query_raw.astype(bf16)
        grads_ref[:, pieces[1]] = grad_key_raw.astype(bf16)
        grads_ref[:, pieces[2]] = grad_value_raw.astype(bf16)
        grads_ref[:, pieces[3]] = grad_gate.astype(bf16)
        carry = carry + jnp.where(lane == head, grad_beta, 0.0)
        carry = carry + jnp.where(lane == heads + head, grad_log, 0.0)

    gain_out[...] = gain_sum
    carry_out[...] = carry
    is_gate = lane >= heads
    grad_small = jnp.where(is_gate, carry * slope_all, carry * beta_all * (1.0 - beta_all))
    if last:
        end = 2 * per_step * (key_dim + value_dim)
        grads_ref[:, end : end + LANES] = jnp.where(lane < 2 * heads, grad_small, 0.0).astype(bf16)
    lanes_out[0:1, :] = jnp.sum(jnp.where(is_gate, carry * gates_all, 0.0), 0, keepdims=True)
    lanes_out[1:2, :] = jnp.sum(grad_small, 0, keepdims=True)
    grads = grads_ref[...]
    outer(x_ref, grads, sum_ref)
    out_copies = spill(chunks, starts_ref, sum_ref, sems.at[0])
    wait_all(copies)
    hidden_out[...] = hidden_ref[...] + dot1(grads, weight_ref[...], "nt")
    wait_all(out_copies)


def ffn_kernel(
    count, starts_ref, x_ref, cot_ref, *refs
):
    gate_pieces = refs[:count]
    down_pieces = refs[count : 2 * count]
    inner_ref, grads_ref, hidden_ref, weight_ref, down_ref, sems = refs[2 * count :]
    hidden = inner_ref.shape[1]
    copies = fetch(gate_pieces, starts_ref, weight_ref, sems.at[0], slice(0, 2 * hidden))
    down_copies = fetch(down_pieces, starts_ref, down_ref, sems.at[1], slice(0, hidden))
    wait_all(copies)
    rows = x_ref[...]
    gate_pre = dot1(rows, weight_ref[:, :hidden])
    up_pre = dot1(rows, weight_ref[:, hidden:])
    sigma = jax.nn.sigmoid(gate_pre)
    gate_act = gate_pre * sigma
    inner_ref[...] = (gate_act * up_pre).astype(bf16)
    wait_all(down_copies)
    grad_inner = dot1(cot_ref[...], down_ref[...])
    grads_ref[:, :hidden] = (grad_inner * up_pre * silu_slope(gate_pre, sigma)).astype(bf16)
    grads_ref[:, hidden:] = (grad_inner * gate_act).astype(bf16)
    hidden_ref[...] = dot1(grads_ref[...], weight_ref[...], "nt")


def outer_kernel(count, starts_ref, left_ref, right_ref, *refs):
    chunks = refs[:count]
    sum_ref, sems = refs[count:]
    outer(left_ref, right_ref[...], sum_ref)
    wait_all(spill(chunks, starts_ref, sum_ref, sems))


def branch_kernel(count, starts_ref, left_ref, *refs):
    pieces = refs[:count]
    out_ref, weight_ref, sems = refs[count:]
    copies = fetch(pieces, starts_ref, weight_ref, sems, slice(0, left_ref.shape[1]))
    wait_all(copies)
    out_ref[...] = dot1(left_ref[...], weight_ref[...], "nt")


VMEM_SPEC = pl.BlockSpec(memory_space=pltpu.VMEM)
HBM_SPEC = pl.BlockSpec(memory_space=pl.ANY)
SMEM_SPEC = pl.BlockSpec(memory_space=pltpu.SMEM)


def call(kernel, starts, inside, outside, out_inside, out_outside, scratch):
    shapes = list(out_outside) + list(out_inside)
    return pl.pallas_call(
        kernel,
        in_specs=[SMEM_SPEC] + [VMEM_SPEC] * len(inside) + [HBM_SPEC] * len(outside),
        out_specs=[HBM_SPEC] * len(out_outside) + [VMEM_SPEC] * len(out_inside),
        out_shape=shapes,
        scratch_shapes=scratch,
    )(starts, *inside, *outside)


def shape(dims, dtype):
    return jax.ShapeDtypeStruct(dims, dtype)


def mixer_forward(starts, pieces, rows, lanes, convs, gain, heads, group, per_step):
    length, model = rows.shape
    key_dim = convs[0].shape[1] // per_step
    value_dim = convs[2].shape[1] // per_step
    wide = per_step * value_dim
    width = 2 * per_step * (key_dim + value_dim)
    count = len(pieces)
    return call(
        functools.partial(forward_kernel, heads, group, per_step, key_dim, value_dim, count),
        starts, (rows, lanes, *convs, gain), pieces,
        [
            shape((length, width), f32),
            shape((length, LANES), f32),
            shape((length, wide), bf16),
            shape((length, wide), f32),
            shape((length, wide), f32),
            shape((per_step, length // SUB, SUB, SUB), f32),
        ],
        [],
        [
            pltpu.VMEM((model, width), bf16),
            pltpu.VMEM((model, LANES), bf16),
            pltpu.SemaphoreType.DMA((2, count)),
        ],
    )


def mixer_backward(
    starts, pieces, out_pieces, rows, grad_rows, proj, small, lanes, convs, gain, saved,
    carry, hidden, heads, group, per_step, last,
):
    length, model = rows.shape
    taps = convs[0].shape[0]
    key_dim = convs[0].shape[1] // per_step
    value_dim = convs[2].shape[1] // per_step
    width = proj.shape[1] + (LANES if last else 0)
    count = len(pieces)
    results = call(
        functools.partial(
            backward_kernel, heads, group, per_step, key_dim, value_dim, last, count,
            len(out_pieces),
        ),
        starts,
        (rows, grad_rows, proj, small, lanes, *convs, gain, *saved, carry, hidden),
        list(pieces) + list(out_pieces),
        [
            shape((taps, per_step * key_dim), f32),
            shape((taps, per_step * key_dim), f32),
            shape((taps, per_step * value_dim), f32),
            shape((1, value_dim), f32),
            shape(carry.shape, f32),
            shape((2, LANES), f32),
            shape(hidden.shape, f32),
        ],
        [shape((piece.shape[0], width), bf16) for piece in pieces],
        [
            pltpu.VMEM((model, width), bf16),
            pltpu.VMEM((model, per_step * value_dim), bf16),
            pltpu.VMEM((length, width), bf16),
            pltpu.VMEM((model, width), bf16),
            pltpu.SemaphoreType.DMA((2, count)),
        ],
    )
    return results[:count], results[count : count + 3], results[count + 3 :]


def ffn_pass(starts, gate_pieces, down_pieces, rows, cotangent):
    length, model = rows.shape
    hidden = down_pieces[0].shape[1]
    count = len(gate_pieces)
    return call(
        functools.partial(ffn_kernel, count), starts, (rows, cotangent),
        list(gate_pieces) + list(down_pieces),
        [
            shape((length, hidden), bf16),
            shape((length, 2 * hidden), bf16),
            shape((length, model), f32),
        ],
        [],
        [
            pltpu.VMEM((model, 2 * hidden), bf16),
            pltpu.VMEM((model, hidden), bf16),
            pltpu.SemaphoreType.DMA((2, count)),
        ],
    )


def outer_chunks(starts, like, left, right):
    count = len(like)
    width = right.shape[1]
    return call(
        functools.partial(outer_kernel, count), starts, (left, right), [],
        [], [shape((piece.shape[0], width), bf16) for piece in like],
        [pltpu.VMEM((left.shape[1], width), bf16), pltpu.SemaphoreType.DMA((count,))],
    )


def branch_rows(starts, pieces, left):
    count = len(pieces)
    model = left.shape[0]
    model = sum(piece.shape[0] for piece in pieces)
    return call(
        functools.partial(branch_kernel, count), starts, (left,), pieces,
        [shape((left.shape[0], model), f32)], [],
        [pltpu.VMEM((model, left.shape[1]), bf16), pltpu.SemaphoreType.DMA((count,))],
    )[0]


def rms_rows(inputs, gain):
    wide_rows = inputs.astype(f32)
    inverse = lax.rsqrt(jnp.mean(wide_rows * wide_rows, -1, keepdims=True) + 1e-05)
    normed = wide_rows * inverse
    return (normed, inverse, (normed * gain).astype(bf16))


def rms_back(grad_rows, normed, inverse, gain):
    scaled = grad_rows * gain
    grad_in = inverse * (scaled - normed * jnp.mean(scaled * normed, -1, keepdims=True))
    return (grad_in, jnp.sum(grad_rows * normed, 0))


def by_core(core, mine, other):
    return jnp.where(
        core == 0, jnp.concatenate([mine, other], 0), jnp.concatenate([other, mine], 0)
    )


def spread(core, array):
    return by_core(core, array, jnp.zeros_like(array))


class Ring:
    def __init__(self, axis):
        self.axis = axis
        self.chips = lax.axis_size(axis) // 2
        evens = [chip for chip in range(self.chips) if chip % 2 == 0]
        odds = [chip for chip in range(self.chips) if chip % 2 == 1]
        order = evens + odds[::-1]
        following = [(order[i], order[(i + 1) % self.chips]) for i in range(self.chips)]
        self.moves = [(2 * a, 2 * b) for a, b in following]
        self.moves += [(2 * b + 1, 2 * a + 1) for a, b in following]
        self.plain = self.chips > UNROLLED_CHIPS
        self.pairs = [(i, i ^ 1) for i in range(2 * self.chips)]
        index = lax.axis_index(axis)
        self.core = index % 2
        self.sign = 1 - 2 * self.core
        chip = index // 2
        self.position = jnp.where(
            chip % 2 == 0, chip // 2, self.chips - 1 - (chip - 1) // 2
        )

    def chip_at(self, shift):
        spot = (self.position + shift) % self.chips
        evens = (self.chips + 1) // 2
        return jnp.where(spot < evens, 2 * spot, 2 * (self.chips - 1 - spot) + 1)

    def starts(self, rows):
        if self.plain:
            return jnp.zeros((1,), jnp.int32)
        half = self.chips // 2
        chips = [self.chip_at(0)]
        chips += [self.chip_at(-self.sign * step) for step in range(1, half)]
        chips += [self.chip_at(self.sign * step) for step in range(1, half)]
        far = 2 * rows * self.chip_at(half)
        edges = [2 * rows * chip for chip in chips]
        edges += [far + self.core * rows, far + (1 - self.core) * rows]
        return jnp.stack(edges).astype(jnp.int32)

    def onward(self, array):
        return lax.ppermute(array, self.axis, self.moves)

    def partner(self, array):
        return lax.ppermute(array, self.axis, self.pairs)

    def total(self, array, marks):
        size = 1
        marks = list(marks)
        while size < 2 * self.chips:
            flips = [(i, i ^ size) for i in range(2 * self.chips)]
            if marks:
                array = after(array, marks.pop(0))
            array = array + lax.ppermute(array, self.axis, flips)
            size = 2 * size
        return array


class Gather:
    def __init__(self, ring, shard, *deps):
        shard = after(shard, *deps)
        self.ring = ring
        self.rows = shard.shape[0]
        self.half = ring.chips // 2
        self.step = 0
        self.piece = shard
        if ring.plain:
            self.pieces = [lax.all_gather(shard, ring.axis, axis=0, tiled=True)]
            self.step = self.half
            return
        other = ring.partner(shard)
        self.piece = by_core(ring.core, shard, other)
        self.pieces = [self.piece]
        self.echoes = []

    def advance(self, *deps):
        if self.step == self.half:
            return self
        self.step = self.step + 1
        ring, rows = self.ring, self.rows
        piece = after(self.piece, *deps)
        if self.step == self.half:
            piece = lax.dynamic_slice_in_dim(piece, ring.core * rows, rows, 0)
        piece = ring.onward(piece)
        echo = ring.partner(piece)
        self.pieces.append(piece)
        self.echoes.append(echo)
        self.piece = piece
        return self

    def finish(self):
        while self.step < self.half:
            self.advance()
        if self.ring.plain:
            return self.pieces
        return self.pieces[:-1] + self.echoes[:-1] + [self.pieces[-1], self.echoes[-1]]


class Scatter:
    def __init__(self, ring, chunks):
        self.ring = ring
        self.chunks = chunks
        self.half = ring.chips // 2
        self.step = 0 if ring.plain else self.half
        self.arrived = chunks[0]

    def advance(self, *deps):
        if self.step == 0:
            return self
        ring, half, chunks = self.ring, self.half, self.chunks
        if self.step == half:
            echo = ring.partner(chunks[2 * half])
            moving = chunks[2 * half - 1].astype(f32) + echo.astype(f32)
        else:
            echo = ring.partner(chunks[self.step]).astype(f32)
            arrived = self.arrived.astype(f32)
            if self.step == half - 1:
                arrived = spread(ring.core, arrived)
            moving = chunks[half - 1 + self.step].astype(f32) + echo + arrived
        self.arrived = ring.onward(after(moving.astype(bf16), *deps))
        self.step = self.step - 1
        return self

    def finish(self):
        ring = self.ring
        if ring.plain:
            return lax.psum_scatter(
                self.chunks[0].astype(f32), ring.axis, scatter_dimension=0, tiled=True
            )
        while self.step > 0:
            self.advance()
        arrived = self.arrived.astype(f32)
        if self.half == 1:
            arrived = spread(ring.core, arrived)
        own = self.chunks[0].astype(f32) + arrived
        rows = own.shape[0] // 2
        give = lax.dynamic_slice_in_dim(own, (1 - ring.core) * rows, rows, 0).astype(bf16)
        keep = lax.dynamic_slice_in_dim(own, ring.core * rows, rows, 0)
        return keep + ring.partner(give).astype(f32)


def others_of(array, axis):
    count = lax.axis_size(axis)
    received = []
    for shift in range(1, count):
        moves = [(i, (i + shift) % count) for i in range(count)]
        received.append(lax.ppermute(array, axis, moves))
    return received


def by_index(axis, pieces, dim):
    count = lax.axis_size(axis)
    index = lax.axis_index(axis)
    joined = None
    for value in range(count):
        here = jnp.concatenate([pieces[(value - i) % count] for i in range(count)], dim)
        joined = here if joined is None else jnp.where(index == value, here, joined)
    return joined


def gather_rows(array, axis):
    return by_index(axis, [array] + others_of(array, axis), 0)


def scatter_rows(partial, axis):
    count = lax.axis_size(axis)
    index = lax.axis_index(axis)
    rows = partial.shape[0] // count
    total = lax.dynamic_slice_in_dim(partial, index * rows, rows, 0)
    for shift in range(1, count):
        target = (index + shift) % count
        part = lax.dynamic_slice_in_dim(partial, target * rows, rows, 0).astype(bf16)
        moves = [(i, (i + shift) % count) for i in range(count)]
        total = total + lax.ppermute(part, axis, moves).astype(f32)
    return total


def after(array, *done):
    return lax.optimization_barrier((array, *done))[0] if done else array


def on_device(
    tokens, out_cotangent, seq_lengths, norm_gain1, query_weight, key_weight, value_weight,
    out_gate_weight, beta_weight, decay_weight, conv_query, conv_key, conv_value,
    decay_log_rate, decay_bias, out_gain, out_weight, norm_gain2, ffn_gate_weight,
    ffn_up_weight, ffn_down_weight,
):
    ring = Ring("dp")
    local_rows = tokens.shape[0]
    tensor_index = lax.axis_index("tensor")
    seq_length = seq_lengths[0]
    local_pos = tensor_index * local_rows + jnp.arange(local_rows, dtype=jnp.int32)
    local_mask = (local_pos < seq_length).astype(f32)[:, None]
    key_cols = query_weight.shape[1]
    value_cols = value_weight.shape[1]
    heads = beta_weight.shape[1]
    hidden_cols = ffn_gate_weight.shape[1]
    per_step = max(1, heads // 2)
    groups = heads // per_step
    wide_key = key_cols // groups
    wide_value = value_cols // groups
    grouped = 2 * (wide_key + wide_value)

    def group_of(array, group):
        wide = array.shape[1] // groups
        return array[:, group * wide : (group + 1) * wide]

    starts = ring.starts(query_weight.shape[0])
    proj_weights = (query_weight, key_weight, value_weight, out_gate_weight)
    narrow = jnp.concatenate([beta_weight, decay_weight], 1)
    parts = [group_of(weight, group) for group in range(groups) for weight in proj_weights]
    parts.append(jnp.pad(narrow, ((0, 0), (0, LANES - 2 * heads))))
    proj_joined = jnp.concatenate(parts, 1)
    ffn_joined = jnp.concatenate([ffn_gate_weight, ffn_up_weight], 1)
    normed1, inverse1, hidden1 = rms_rows(tokens, norm_gain1)
    whole1 = gather_rows(hidden1, "tensor")
    grad_local = (local_mask * out_cotangent.astype(f32)).astype(bf16)
    grad_whole = gather_rows(grad_local, "tensor")
    lanes = jnp.pad(
        jnp.stack([decay_log_rate, decay_bias]), ((0, 0), (heads, LANES - 2 * heads))
    )
    gain_wide = out_gain[None]
    convs = [
        tuple(group_of(conv, group) for conv in (conv_query, conv_key, conv_value))
        for group in range(groups)
    ]

    proj_gather = Gather(ring, proj_joined)
    proj_gather.advance().advance()
    out_gather = Gather(ring, out_weight, proj_gather.piece)
    proj_gather.advance()
    out_gather.advance()
    late = proj_gather.piece
    proj_pieces = proj_gather.finish()
    out_pieces = out_gather.finish()
    ffn_gather = Gather(ring, ffn_joined, late)
    down_gather = Gather(ring, ffn_down_weight, late)
    ffn_pieces = ffn_gather.finish()
    down_pieces = down_gather.finish()
    projections = []
    halves = []
    saved = []
    for group in range(groups):
        proj, small, half, *kept = mixer_forward(
            starts, proj_pieces, whole1, lanes, convs[group], gain_wide, heads, group, per_step
        )
        projections.append(proj)
        halves.append(half)
        saved.append(kept)
    mixed_half = jnp.concatenate(halves, 1)
    branch = scatter_rows(branch_rows(starts, out_pieces, mixed_half), "tensor")
    residual = tokens.astype(f32) + branch
    normed2, inverse2, hidden2 = rms_rows(residual, norm_gain2)
    whole2 = gather_rows(hidden2, "tensor")

    inner_act, grad_pre_both, partial_hidden2 = ffn_pass(
        starts, ffn_pieces, down_pieces, whole2, grad_whole
    )
    grad_hidden2 = scatter_rows(partial_hidden2, "tensor")
    ffn_chunks = outer_chunks(starts, ffn_pieces, whole2, grad_pre_both)
    down_chunks = outer_chunks(starts, ffn_pieces, grad_whole, inner_act)
    ffn_scatter = Scatter(ring, ffn_chunks)
    down_scatter = Scatter(ring, down_chunks)
    grad_normed2, second_gain_gradient = rms_back(grad_hidden2, normed2, inverse2, norm_gain2)
    grad_residual = local_mask * out_cotangent.astype(f32) + grad_normed2
    grad_whole1 = gather_rows(grad_residual.astype(bf16), "tensor")
    ffn_branch = scatter_rows(
        branch_rows(starts, down_pieces, after(inner_act, grad_residual)), "tensor"
    )
    output = (local_mask * (residual + ffn_branch)).astype(bf16)
    down_shard = down_scatter.finish()
    ffn_shard = ffn_scatter.finish()
    out_chunks = outer_chunks(starts, out_pieces, grad_whole1, mixed_half)
    out_shard = Scatter(ring, out_chunks).finish()
    carry = jnp.zeros((whole1.shape[0], LANES), f32)
    partial_hidden = jnp.zeros(whole1.shape, f32)
    conv_grads = []
    gain_sum = 0.0
    scatters = []
    for group in range(groups):
        chunks, conv_grad, (gain_part, carry, lane_sums, partial_hidden) = mixer_backward(
            starts, proj_pieces, out_pieces, whole1, grad_whole1, projections[group], small,
            lanes, convs[group], gain_wide, saved[group], carry, partial_hidden, heads, group,
            per_step, group == groups - 1,
        )
        conv_grads.append(conv_grad)
        gain_sum = gain_sum + gain_part
        scatters.append(Scatter(ring, chunks))
    grad_hidden1 = scatter_rows(partial_hidden, "tensor")
    grad_normed1, first_gain_gradient = rms_back(grad_hidden1, normed1, inverse1, norm_gain1)
    grad_tokens = (grad_residual + grad_normed1).astype(bf16)
    marks = []
    while scatters[-1].step > 0:
        scatters[-1].advance()
        marks.append(scatters[-1].arrived)
    proj_shards = [scatter.finish() for scatter in scatters]
    edges = [0, wide_key, 2 * wide_key, 2 * wide_key + wide_value, grouped]
    mixer_grads = [
        jnp.concatenate([shard[:, edges[i] : edges[i + 1]] for shard in proj_shards], 1)
        for i in range(4)
    ]
    mixer_grads.append(proj_shards[-1][:, grouped : grouped + heads])
    mixer_grads.append(proj_shards[-1][:, grouped + heads : grouped + 2 * heads])
    ffn_grads = [ffn_shard[:, :hidden_cols], ffn_shard[:, hidden_cols:]]
    grad_conv_query, grad_conv_key, grad_conv_value = [
        jnp.concatenate([conv_grad[i] for conv_grad in conv_grads], 1) for i in range(3)
    ]

    taps = conv_query.shape[0]
    blocks = [
        jnp.concatenate([grad_conv_query, grad_conv_key], 1),
        grad_conv_value,
        first_gain_gradient[None],
        second_gain_gradient[None],
        gain_sum,
        lane_sums[:, : 2 * heads],
    ]
    wide = max(block.shape[1] for block in blocks)
    tall = sum(block.shape[0] for block in blocks)
    blocks = [jnp.pad(block, ((0, 0), (0, wide - block.shape[1]))) for block in blocks]
    blocks.append(jnp.zeros((-tall % 8, wide), f32))
    packed = ring.total(jnp.concatenate(blocks, 0), marks)
    pieces = [packed] + others_of(packed, "tensor")
    summed = pieces[0]
    for member in pieces[1:]:
        summed = summed + member

    def joined(row, rows, start, cols):
        parts = [member[row : row + rows, start : start + cols] for member in pieces]
        return by_index("tensor", parts, 1)

    gain_row = 2 * taps
    return (
        output,
        grad_tokens,
        summed[gain_row, : norm_gain1.shape[0]],
        mixer_grads[0],
        mixer_grads[1],
        mixer_grads[2],
        mixer_grads[3],
        mixer_grads[4],
        mixer_grads[5],
        joined(0, taps, 0, key_cols),
        joined(0, taps, key_cols, key_cols),
        joined(taps, taps, 0, value_cols),
        joined(gain_row + 3, 1, heads, heads)[0],
        joined(gain_row + 4, 1, heads, heads)[0],
        summed[gain_row + 2, : out_gain.shape[0]],
        out_shard,
        summed[gain_row + 1, : norm_gain2.shape[0]],
        ffn_grads[0],
        ffn_grads[1],
        down_shard,
    )


def solution(mesh):
    in_specs = (
        P(("dp", "tensor"), None),
        P(("dp", "tensor"), None),
        P("dp"),
        P(),
        P("dp", "tensor"),
        P("dp", "tensor"),
        P("dp", "tensor"),
        P("dp", "tensor"),
        P("dp", "tensor"),
        P("dp", "tensor"),
        P(None, "tensor"),
        P(None, "tensor"),
        P(None, "tensor"),
        P("tensor"),
        P("tensor"),
        P(),
        P("dp", "tensor"),
        P(),
        P("dp", "tensor"),
        P("dp", "tensor"),
        P("dp", "tensor"),
    )
    out_specs = (
        P(("dp", "tensor"), None),
        P(("dp", "tensor"), None),
        P(),
        P("dp", "tensor"),
        P("dp", "tensor"),
        P("dp", "tensor"),
        P("dp", "tensor"),
        P("dp", "tensor"),
        P("dp", "tensor"),
        P(),
        P(),
        P(),
        P(),
        P(),
        P(),
        P("dp", "tensor"),
        P(),
        P("dp", "tensor"),
        P("dp", "tensor"),
        P("dp", "tensor"),
    )

    return jax.shard_map(
        on_device, mesh=mesh, in_specs=in_specs, out_specs=out_specs, check_vma=False
    )
```

```python
import functools

import jax
import jax.numpy as jnp
from jax import lax
from jax.experimental import pallas as pl
from jax.experimental.pallas import tpu as pltpu
from jax.sharding import PartitionSpec as P


SUB = 128
LANES = 128
UNROLLED_CHIPS = 16
bf16 = jnp.bfloat16
f32 = jnp.float32


def dims_of(kind):
    return {
        "nn": (((1,), (0,)), ((), ())),
        "nt": (((1,), (1,)), ((), ())),
        "tn": (((0,), (0,)), ((), ())),
    }[kind]


def dot1(left, right, kind="nn"):
    return lax.dot_general(left, right, dims_of(kind), preferred_element_type=f32)


def cut(array):
    high = array.astype(bf16)
    return (high, (array - high.astype(f32)).astype(bf16))


def dot3(left, right, kind="nn"):
    return (
        dot1(left[0], right[0], kind)
        + dot1(left[0], right[1], kind)
        + dot1(left[1], right[0], kind)
    )


def shift_down(array, amount):
    if amount == 0:
        return array
    rows = lax.broadcasted_iota(jnp.int32, array.shape, 0)
    return jnp.where(rows >= amount, pltpu.roll(array, amount, 0), 0.0)


def shift_up(array, amount):
    if amount == 0:
        return array
    length = array.shape[0]
    rows = lax.broadcasted_iota(jnp.int32, array.shape, 0)
    return jnp.where(rows < length - amount, pltpu.roll(array, length - amount, 0), 0.0)


def conv_rows(projected, kernel):
    taps = kernel.shape[0]
    summed = kernel[taps - 1 : taps] * projected
    for offset in range(1, taps):
        tap = taps - 1 - offset
        summed = summed + kernel[tap : tap + 1] * shift_down(projected, offset)
    return summed


def conv_back(grad_conv, projected, kernel):
    taps = kernel.shape[0]
    grad_proj = kernel[taps - 1 : taps] * grad_conv
    for offset in range(1, taps):
        tap = taps - 1 - offset
        grad_proj = grad_proj + kernel[tap : tap + 1] * shift_up(grad_conv, offset)
    terms = []
    for tap in range(taps):
        moved = shift_down(projected, taps - 1 - tap)
        terms.append(jnp.sum(grad_conv * moved, 0, keepdims=True))
    return grad_proj, jnp.concatenate(terms, 0)


def silu_slope(values, sigma):
    return sigma * (1.0 + values * (1.0 - sigma))


def gate_rows(small, lanes_ref, heads):
    lane = lax.broadcasted_iota(jnp.int32, small.shape, 1)
    rate = jnp.exp(lanes_ref[0:1, :])
    shifted = small + lanes_ref[1:2, :]
    soft = jnp.maximum(shifted, 0.0) + jnp.log1p(jnp.exp(-jnp.abs(shifted)))
    gates = jnp.where(lane >= heads, -rate * soft, 0.0)
    slope = jnp.where(lane >= heads, -rate * jax.nn.sigmoid(shifted), 0.0)
    return jax.nn.sigmoid(small), gates, slope


def sum_gates(gates):
    length = gates.shape[0]
    row = lax.broadcasted_iota(jnp.int32, (length, length), 0)
    col = lax.broadcasted_iota(jnp.int32, (length, length), 1)
    lower = (row >= col).astype(f32)
    upper = (row <= col).astype(f32)
    kwargs = dict(precision=lax.Precision.HIGHEST, preferred_element_type=f32)
    by_row = lax.dot_general(lower, gates, dims_of("nn"), **kwargs)
    by_col = lax.dot_general(gates, upper, dims_of("tn"), **kwargs)
    return by_row, by_col


def lane_pick(array, index):
    lane = lax.broadcasted_iota(jnp.int32, array.shape, 1)
    return jnp.sum(jnp.where(lane == index, array, 0.0), 1, keepdims=True)


def row_pick(array, index):
    row = lax.broadcasted_iota(jnp.int32, array.shape, 0)
    return jnp.sum(jnp.where(row == index, array, 0.0), 0, keepdims=True)


def decay_square(cum_col, cum_row):
    length = cum_col.shape[0]
    row = lax.broadcasted_iota(jnp.int32, (length, length), 0)
    col = lax.broadcasted_iota(jnp.int32, (length, length), 1)
    keep = row >= col
    square = jnp.where(keep, jnp.exp(jnp.where(keep, cum_col - cum_row, 0.0)), 0.0)
    return square, keep, row > col


def unit_rows(raw, kernel):
    conv = conv_rows(raw, kernel)
    sigma = jax.nn.sigmoid(conv)
    act = conv * sigma
    inverse = lax.rsqrt(jnp.sum(act * act, -1, keepdims=True) + 1e-06)
    return conv, sigma, act, inverse


def fetch(pieces, starts_ref, target, sems, segments):
    copies = []
    for j, (source, place, width) in enumerate(segments):
        for i, piece in enumerate(pieces):
            rows = piece.shape[0]
            start = pl.multiple_of(starts_ref[i], rows)
            copies.append(
                pltpu.make_async_copy(
                    piece.at[:, source : source + width],
                    target.at[pl.ds(start, rows), place : place + width],
                    sems.at[j, i],
                )
            )
    for copy in copies:
        copy.start()
    return copies


def proj_segments(group, groups, wide_key, wide_value):
    key_cols = groups * wide_key
    value_cols = groups * wide_value
    return [
        (group * wide_key, 0, wide_key),
        (key_cols + group * wide_key, wide_key, wide_key),
        (2 * key_cols + group * wide_value, 2 * wide_key, wide_value),
        (2 * key_cols + value_cols + group * wide_value, 2 * wide_key + wide_value, wide_value),
    ]


def spill(chunks, starts_ref, source, sems):
    copies = []
    for i, chunk in enumerate(chunks):
        rows = chunk.shape[0]
        start = pl.multiple_of(starts_ref[i], rows)
        copies.append(pltpu.make_async_copy(source.at[pl.ds(start, rows), :], chunk, sems.at[i]))
    for copy in copies:
        copy.start()
    return copies


def wait_all(copies):
    for copy in copies:
        copy.wait()


def outer(left_ref, right, target_ref, place):
    cols = slice(place, place + right.shape[1])
    total = left_ref.shape[1]
    step = 256 if total % 256 == 0 else total
    for start in range(0, total, step):
        span = slice(start, start + step)
        target_ref[span, cols] = dot1(left_ref[:, span], right, "tn").astype(bf16)


def head_cuts(local, per_step, key_dim, value_dim):
    wide_key = per_step * key_dim
    wide_value = per_step * value_dim
    kcut = slice(local * key_dim, (local + 1) * key_dim)
    vcut = slice(local * value_dim, (local + 1) * value_dim)
    starts = (
        local * key_dim,
        wide_key + local * key_dim,
        2 * wide_key + local * value_dim,
        2 * wide_key + wide_value + local * value_dim,
    )
    widths = (key_dim, key_dim, value_dim, value_dim)
    pieces = [slice(start, start + width) for start, width in zip(starts, widths)]
    return kcut, vcut, pieces


def forward_kernel(
    heads, group, per_step, key_dim, value_dim, count,
    starts_ref, x_ref, lanes_ref, conv_query_ref, conv_key_ref, conv_value_ref, gain_ref, *refs
):
    pieces = refs[:count]
    proj_ref, small_ref, half_ref, mixed_ref, update_ref, inverse_ref = refs[count : count + 6]
    weight_ref, small_weight_ref, sems = refs[count + 6 :]
    end = 2 * heads * (key_dim + value_dim)
    segments = proj_segments(
        group, heads // per_step, per_step * key_dim, per_step * value_dim
    )
    copies = fetch(pieces, starts_ref, weight_ref, sems.at[0:4], segments)
    small_cols = [(end, 0, LANES)]
    copies += fetch(pieces, starts_ref, small_weight_ref, sems.at[4:5], small_cols)
    wait_all(copies)
    small_ref[...] = dot1(x_ref[...], small_weight_ref[...])
    proj_ref[...] = dot1(x_ref[...], weight_ref[...])
    length = proj_ref.shape[0]
    blocks = length // SUB
    beta_all, gates_all, _ = gate_rows(small_ref[...], lanes_ref, heads)
    cum_all, cum_rows = sum_gates(gates_all)
    sub_row = lax.broadcasted_iota(jnp.int32, (SUB, SUB), 0)
    sub_col = lax.broadcasted_iota(jnp.int32, (SUB, SUB), 1)
    state = []
    for local in range(per_step):
        head = group * per_step + local
        kcut, vcut, pieces = head_cuts(local, per_step, key_dim, value_dim)
        _, _, query_act, query_inv = unit_rows(proj_ref[:, pieces[0]], conv_query_ref[:, kcut])
        query = query_act * query_inv * key_dim ** (-0.5)
        _, _, key_act, key_inv = unit_rows(proj_ref[:, pieces[1]], conv_key_ref[:, kcut])
        key = key_act * key_inv
        value_conv = conv_rows(proj_ref[:, pieces[2]], conv_value_ref[:, vcut])
        value = value_conv * jax.nn.sigmoid(value_conv)
        beta = lane_pick(beta_all, head)
        decay, _, strict = decay_square(
            lane_pick(cum_all, heads + head), row_pick(cum_rows, heads + head)
        )
        key_parts = cut(key)
        coupling = jnp.where(strict, beta * dot3(key_parts, key_parts, "nt") * decay, 0.0)
        mix = dot3(cut(query), key_parts, "nt") * decay
        state.append((coupling, mix, beta * value))
    inverses = []
    for coupling, _, _ in state:
        parts = []
        for block in range(blocks):
            span = slice(block * SUB, (block + 1) * SUB)
            parts.append(coupling[span, span])
        inverses.append(parts)
    squares = [[part for part in parts] for parts in inverses]
    eye = (sub_row == sub_col).astype(f32)
    size = 1
    current = [[None] * blocks for _ in state]
    while size < SUB:
        member = ((sub_row // (2 * size)) == (sub_col // (2 * size))) & (
            (sub_row // size) != (sub_col // size)
        )
        for h in range(per_step):
            for block in range(blocks):
                cross = jnp.where(member, squares[h][block], 0.0)
                if size == 1:
                    current[h][block] = eye - cross
                else:
                    now = cut(current[h][block])
                    inner = dot3(cut(cross), now)
                    current[h][block] = current[h][block] - dot3(now, cut(inner))
        size = 2 * size
    for local in range(per_step):
        _, vcut, pieces = head_cuts(local, per_step, key_dim, value_dim)
        coupling, mix, target = state[local]
        solved = []
        for block in range(blocks):
            span = slice(block * SUB, (block + 1) * SUB)
            rest = target[span]
            for before in range(block):
                past = slice(before * SUB, (before + 1) * SUB)
                rest = rest - dot3(cut(coupling[span, past]), cut(solved[before]))
            solved.append(dot3(cut(current[local][block]), cut(rest)))
            inverse_ref[local, block] = current[local][block]
        updates = jnp.concatenate(solved, 0)
        mixed = dot3(cut(mix), cut(updates))
        update_ref[:, vcut] = updates
        mixed_ref[:, vcut] = mixed
        inverse = lax.rsqrt(jnp.mean(mixed * mixed, -1, keepdims=True) + 1e-05)
        gate = proj_ref[:, pieces[3]]
        half_ref[:, vcut] = (
            mixed * inverse * gain_ref[...] * (gate * jax.nn.sigmoid(gate))
        ).astype(bf16)


def unit_back(grad, conv, sigma, act, inverse, scale):
    inner = jnp.sum(grad * act, -1, keepdims=True)
    grad_act = scale * inverse * (grad - act * (inverse * inverse) * inner)
    return grad_act * silu_slope(conv, sigma)


def backward_kernel(
    heads, group, per_step, key_dim, value_dim, last, count,
    starts_ref, x_ref, grad_rows_ref, proj_ref, small_ref, lanes_ref,
    conv_query_ref, conv_key_ref, conv_value_ref, gain_ref,
    mixed_ref, update_ref, inverse_ref, *refs
):
    taken = refs[: 2 if group > 0 else heads // per_step]
    refs = refs[len(taken) :]
    pieces = refs[:count]
    refs = refs[count:]
    chunks = refs[:count]
    conv_query_out, conv_key_out, conv_value_out, gain_out, carry_out, lanes_out, hidden_out = refs[
        count : count + 7
    ]
    weight_ref, out_weight_ref, grads_ref, sum_ref, sems, out_sems = refs[count + 7 :]
    width = grads_ref.shape[1]
    value_width = mixed_ref.shape[1]
    grouped = 2 * per_step * (key_dim + value_dim)
    end = 2 * heads * (key_dim + value_dim)
    out_copies = fetch(
        pieces, starts_ref, out_weight_ref, out_sems,
        [(end + LANES + group * value_width, 0, value_width)],
    )
    segments = proj_segments(
        group, heads // per_step, per_step * key_dim, per_step * value_dim
    )
    if last:
        segments.append((end, grouped, LANES))
    copies = fetch(pieces, starts_ref, weight_ref, sems, segments)
    wait_all(out_copies)
    grad_all = dot1(grad_rows_ref[...], out_weight_ref[...])
    length = proj_ref.shape[0]
    blocks = length // SUB
    small = small_ref[...]
    beta_all, gates_all, slope_all = gate_rows(small, lanes_ref, heads)
    cum_all, cum_rows = sum_gates(gates_all)
    lane = lax.broadcasted_iota(jnp.int32, small.shape, 1)
    upper = (
        lax.broadcasted_iota(jnp.int32, (length, length), 0)
        <= lax.broadcasted_iota(jnp.int32, (length, length), 1)
    ).astype(bf16)

    carry = taken[0][...] if group > 0 else jnp.zeros(small.shape, f32)
    gain_sum = jnp.zeros((1, value_dim), f32)
    for local in range(per_step):
        head = group * per_step + local
        kcut, vcut, pieces = head_cuts(local, per_step, key_dim, value_dim)
        scale = key_dim ** (-0.5)
        query_raw = proj_ref[:, pieces[0]]
        key_raw = proj_ref[:, pieces[1]]
        value_raw = proj_ref[:, pieces[2]]
        query_conv, query_sigma, query_act, query_inv = unit_rows(
            query_raw, conv_query_ref[:, kcut]
        )
        query = query_act * query_inv * scale
        key_conv, key_sigma, key_act, key_inv = unit_rows(key_raw, conv_key_ref[:, kcut])
        key = key_act * key_inv
        value_conv = conv_rows(value_raw, conv_value_ref[:, vcut])
        value_sigma = jax.nn.sigmoid(value_conv)
        value = value_conv * value_sigma
        mixed = mixed_ref[:, vcut]
        inverse = lax.rsqrt(jnp.mean(mixed * mixed, -1, keepdims=True) + 1e-05)
        gate = proj_ref[:, pieces[3]]
        gate_sigma = jax.nn.sigmoid(gate)
        gain = gain_ref[...]
        normed = mixed * inverse
        grad_out = grad_all[:, vcut]
        through = grad_out * normed
        grad_gate = through * gain * silu_slope(gate, gate_sigma)
        swish = gate * gate_sigma
        gain_sum = gain_sum + jnp.sum(through * swish, 0, keepdims=True)
        grad_normed = grad_out * gain * swish
        grad_mixed = inverse * (
            grad_normed - normed * jnp.mean(grad_normed * normed, -1, keepdims=True)
        )
        beta = lane_pick(beta_all, head)
        decay, keep, strict = decay_square(
            lane_pick(cum_all, heads + head), row_pick(cum_rows, heads + head)
        )
        key_parts = cut(key)
        query_parts = cut(query)
        pair = dot3(key_parts, key_parts, "nt") * decay
        coupling = jnp.where(strict, beta * pair, 0.0)
        mix = dot3(query_parts, key_parts, "nt") * decay
        updates = cut(update_ref[:, vcut])
        grad_parts = cut(grad_mixed)
        grad_mix = jnp.where(keep, dot3(grad_parts, updates, "nt"), 0.0)
        grad_updates = dot3(cut(mix), grad_parts, "tn")
        solved = [None] * blocks
        for block in reversed(range(blocks)):
            span = slice(block * SUB, (block + 1) * SUB)
            rest = grad_updates[span]
            for after in range(block + 1, blocks):
                later = slice(after * SUB, (after + 1) * SUB)
                rest = rest - dot3(cut(coupling[later, span]), cut(solved[after]), "tn")
            solved[block] = dot3(cut(inverse_ref[local, block]), cut(rest), "tn")
        grad_target = jnp.concatenate(solved, 0)
        grad_coupling = jnp.where(strict, -dot3(cut(grad_target), updates, "nt"), 0.0)
        grad_value = beta * grad_target
        grad_beta = jnp.sum(grad_target * value, -1, keepdims=True) + jnp.sum(
            grad_coupling * pair, -1, keepdims=True
        )
        flow = cut(grad_coupling * coupling + grad_mix * mix)
        run = dot1(upper, flow[0]) + dot1(upper, flow[1])
        grad_log = jnp.sum(jnp.where(strict, run, 0.0), -1, keepdims=True)
        grad_pair = cut(grad_coupling * beta * decay)
        grad_cross = cut(grad_mix * decay)
        grad_query = dot3(grad_cross, key_parts)
        grad_key = (
            dot3(grad_cross, query_parts, "tn")
            + dot3(grad_pair, key_parts)
            + dot3(grad_pair, key_parts, "tn")
        )
        grad_query_raw, grad_conv = conv_back(
            unit_back(grad_query, query_conv, query_sigma, query_act, query_inv, scale),
            query_raw, conv_query_ref[:, kcut],
        )
        conv_query_out[:, kcut] = grad_conv
        grad_key_raw, grad_conv = conv_back(
            unit_back(grad_key, key_conv, key_sigma, key_act, key_inv, 1.0),
            key_raw, conv_key_ref[:, kcut],
        )
        conv_key_out[:, kcut] = grad_conv
        grad_value_raw, grad_conv = conv_back(
            grad_value * silu_slope(value_conv, value_sigma), value_raw, conv_value_ref[:, vcut]
        )
        conv_value_out[:, vcut] = grad_conv
        grads_ref[:, pieces[0]] = grad_query_raw.astype(bf16)
        grads_ref[:, pieces[1]] = grad_key_raw.astype(bf16)
        grads_ref[:, pieces[2]] = grad_value_raw.astype(bf16)
        grads_ref[:, pieces[3]] = grad_gate.astype(bf16)
        carry = carry + jnp.where(lane == head, grad_beta, 0.0)
        carry = carry + jnp.where(lane == heads + head, grad_log, 0.0)

    gain_out[...] = gain_sum
    carry_out[...] = carry
    is_gate = lane >= heads
    grad_small = jnp.where(is_gate, carry * slope_all, carry * beta_all * (1.0 - beta_all))
    if last:
        grads_ref[:, grouped : grouped + LANES] = jnp.where(lane < 2 * heads, grad_small, 0.0).astype(bf16)
    lanes_out[0:1, :] = jnp.sum(jnp.where(is_gate, carry * gates_all, 0.0), 0, keepdims=True)
    lanes_out[1:2, :] = jnp.sum(grad_small, 0, keepdims=True)
    grads = grads_ref[...]
    outer(x_ref, grads, sum_ref, 0)
    if group == 0:
        for i, half_ref in enumerate(taken):
            outer(grad_rows_ref, half_ref[...], sum_ref, width + i * value_width)
    out_copies = spill(chunks, starts_ref, sum_ref, out_sems.at[0])
    wait_all(copies)
    hidden = dot1(grads, weight_ref[...], "nt")
    hidden_out[...] = taken[1][...] + hidden if group > 0 else hidden
    wait_all(out_copies)


def ffn_kernel(count, starts_ref, x_ref, cot_ref, *refs):
    pieces = refs[:count]
    down_pieces = refs[count : 2 * count]
    inner_ref, grads_ref, hidden_ref, weight_ref, sems = refs[2 * count :]
    hidden = inner_ref.shape[1]
    copies = fetch(pieces, starts_ref, weight_ref, sems.at[0:1], [(0, 0, 2 * hidden)])
    down_cols = [(0, 2 * hidden, hidden)]
    down_copies = fetch(down_pieces, starts_ref, weight_ref, sems.at[1:2], down_cols)
    wait_all(copies)
    rows = x_ref[...]
    gate_pre = dot1(rows, weight_ref[:, :hidden])
    up_pre = dot1(rows, weight_ref[:, hidden : 2 * hidden])
    sigma = jax.nn.sigmoid(gate_pre)
    gate_act = gate_pre * sigma
    inner_ref[...] = (gate_act * up_pre).astype(bf16)
    wait_all(down_copies)
    grad_inner = dot1(cot_ref[...], weight_ref[:, 2 * hidden :])
    grads_ref[:, :hidden] = (grad_inner * up_pre * silu_slope(gate_pre, sigma)).astype(bf16)
    grads_ref[:, hidden:] = (grad_inner * gate_act).astype(bf16)
    hidden_ref[...] = dot1(grads_ref[...], weight_ref[:, : 2 * hidden], "nt")


def outer_kernel(count, starts_ref, *refs):
    pairs = (len(refs) - count - 2) // 2
    operands = refs[: 2 * pairs]
    chunks = refs[2 * pairs : 2 * pairs + count]
    sum_ref, sems = refs[2 * pairs + count :]
    place = 0
    for i in range(pairs):
        right = operands[2 * i + 1][...]
        outer(operands[2 * i], right, sum_ref, place)
        place = place + right.shape[1]
    wait_all(spill(chunks, starts_ref, sum_ref, sems))


def branch_kernel(count, first, starts_ref, *refs):
    lefts = refs[: len(refs) - count - 3]
    pieces = refs[len(lefts) : len(lefts) + count]
    out_ref, weight_ref, sems = refs[len(lefts) + count :]
    width = weight_ref.shape[1]
    wait_all(fetch(pieces, starts_ref, weight_ref, sems, [(first, 0, width)]))
    total = None
    place = 0
    for left_ref in lefts:
        cols = slice(place, place + left_ref.shape[1])
        part = dot1(left_ref[...], weight_ref[:, cols], "nt")
        total = part if total is None else total + part
        place = place + left_ref.shape[1]
    out_ref[...] = total


VMEM_SPEC = pl.BlockSpec(memory_space=pltpu.VMEM)
HBM_SPEC = pl.BlockSpec(memory_space=pl.ANY)
SMEM_SPEC = pl.BlockSpec(memory_space=pltpu.SMEM)


def call(kernel, starts, inside, outside, out_inside, out_outside, scratch):
    shapes = list(out_outside) + list(out_inside)
    return pl.pallas_call(
        kernel,
        in_specs=[SMEM_SPEC] + [VMEM_SPEC] * len(inside) + [HBM_SPEC] * len(outside),
        out_specs=[HBM_SPEC] * len(out_outside) + [VMEM_SPEC] * len(out_inside),
        out_shape=shapes,
        scratch_shapes=scratch,
    )(starts, *inside, *outside)


def shape(dims, dtype):
    return jax.ShapeDtypeStruct(dims, dtype)


def mixer_forward(starts, pieces, rows, lanes, convs, gain, heads, group, per_step):
    length, model = rows.shape
    key_dim = convs[0].shape[1] // per_step
    value_dim = convs[2].shape[1] // per_step
    wide = per_step * value_dim
    width = 2 * per_step * (key_dim + value_dim)
    count = len(pieces)
    return call(
        functools.partial(forward_kernel, heads, group, per_step, key_dim, value_dim, count),
        starts, (rows, lanes, *convs, gain), pieces,
        [
            shape((length, width), f32),
            shape((length, LANES), f32),
            shape((length, wide), bf16),
            shape((length, wide), f32),
            shape((length, wide), f32),
            shape((per_step, length // SUB, SUB, SUB), f32),
        ],
        [],
        [
            pltpu.VMEM((model, width), bf16),
            pltpu.VMEM((model, LANES), bf16),
            pltpu.SemaphoreType.DMA((5, count)),
        ],
    )


def mixer_backward(
    starts, pieces, rows, grad_rows, proj, small, lanes, convs, gain, saved,
    taken, heads, group, per_step, last,
):
    length, model = rows.shape
    taps = convs[0].shape[0]
    key_dim = convs[0].shape[1] // per_step
    value_dim = convs[2].shape[1] // per_step
    width = proj.shape[1] + (LANES if last else 0)
    extra = sum(half.shape[1] for half in taken) if group == 0 else 0
    count = len(pieces)
    results = call(
        functools.partial(
            backward_kernel, heads, group, per_step, key_dim, value_dim, last, count
        ),
        starts,
        (rows, grad_rows, proj, small, lanes, *convs, gain, *saved, *taken),
        pieces,
        [
            shape((taps, per_step * key_dim), f32),
            shape((taps, per_step * key_dim), f32),
            shape((taps, per_step * value_dim), f32),
            shape((1, value_dim), f32),
            shape((length, LANES), f32),
            shape((2, LANES), f32),
            shape((length, model), f32),
        ],
        [shape((piece.shape[0], width + extra), bf16) for piece in pieces],
        [
            pltpu.VMEM((model, width), bf16),
            pltpu.VMEM((model, per_step * value_dim), bf16),
            pltpu.VMEM((length, width), bf16),
            pltpu.VMEM((model, width + extra), bf16),
            pltpu.SemaphoreType.DMA((5, count)),
            pltpu.SemaphoreType.DMA((1, count)),
        ],
    )
    return results[:count], results[count : count + 3], results[count + 3 :]


def ffn_pass(starts, pieces, down_pieces, rows, cotangent):
    length, model = rows.shape
    hidden = down_pieces[0].shape[1]
    count = len(pieces)
    return call(
        functools.partial(ffn_kernel, count), starts, (rows, cotangent),
        list(pieces) + list(down_pieces),
        [
            shape((length, hidden), bf16),
            shape((length, 2 * hidden), bf16),
            shape((length, model), f32),
        ],
        [],
        [pltpu.VMEM((model, 3 * hidden), bf16), pltpu.SemaphoreType.DMA((2, count))],
    )


def outer_chunks(starts, like, *operands):
    count = len(like)
    width = sum(right.shape[1] for right in operands[1::2])
    return call(
        functools.partial(outer_kernel, count), starts, operands, [],
        [], [shape((piece.shape[0], width), bf16) for piece in like],
        [pltpu.VMEM((operands[0].shape[1], width), bf16), pltpu.SemaphoreType.DMA((count,))],
    )


def branch_rows(starts, pieces, first, *lefts):
    count = len(pieces)
    model = sum(piece.shape[0] for piece in pieces)
    width = sum(left.shape[1] for left in lefts)
    return call(
        functools.partial(branch_kernel, count, first), starts, lefts, pieces,
        [shape((lefts[0].shape[0], model), f32)], [],
        [pltpu.VMEM((model, width), bf16), pltpu.SemaphoreType.DMA((1, count))],
    )[0]


def rms_rows(inputs, gain):
    wide_rows = inputs.astype(f32)
    inverse = lax.rsqrt(jnp.mean(wide_rows * wide_rows, -1, keepdims=True) + 1e-05)
    normed = wide_rows * inverse
    return (normed, inverse, (normed * gain).astype(bf16))


def rms_back(grad_rows, normed, inverse, gain):
    scaled = grad_rows * gain
    grad_in = inverse * (scaled - normed * jnp.mean(scaled * normed, -1, keepdims=True))
    return (grad_in, jnp.sum(grad_rows * normed, 0))


def by_core(core, mine, other):
    return jnp.where(
        core == 0, jnp.concatenate([mine, other], 0), jnp.concatenate([other, mine], 0)
    )


def spread(core, array):
    return by_core(core, array, jnp.zeros_like(array))


class Ring:
    def __init__(self, axis):
        self.axis = axis
        self.chips = lax.axis_size(axis) // 2
        evens = [chip for chip in range(self.chips) if chip % 2 == 0]
        odds = [chip for chip in range(self.chips) if chip % 2 == 1]
        order = evens + odds[::-1]
        following = [(order[i], order[(i + 1) % self.chips]) for i in range(self.chips)]
        self.moves = [(2 * a, 2 * b) for a, b in following]
        self.moves += [(2 * b + 1, 2 * a + 1) for a, b in following]
        self.plain = self.chips > UNROLLED_CHIPS
        self.pairs = [(i, i ^ 1) for i in range(2 * self.chips)]
        index = lax.axis_index(axis)
        self.core = index % 2
        self.sign = 1 - 2 * self.core
        chip = index // 2
        self.position = jnp.where(
            chip % 2 == 0, chip // 2, self.chips - 1 - (chip - 1) // 2
        )

    def chip_at(self, shift):
        spot = (self.position + shift) % self.chips
        evens = (self.chips + 1) // 2
        return jnp.where(spot < evens, 2 * spot, 2 * (self.chips - 1 - spot) + 1)

    def starts(self, rows):
        if self.plain:
            return jnp.zeros((1,), jnp.int32)
        half = self.chips // 2
        chips = [self.chip_at(0)]
        chips += [self.chip_at(-self.sign * step) for step in range(1, half)]
        chips += [self.chip_at(self.sign * step) for step in range(1, half)]
        far = 2 * rows * self.chip_at(half)
        edges = [2 * rows * chip for chip in chips]
        edges += [far + self.core * rows, far + (1 - self.core) * rows]
        return jnp.stack(edges).astype(jnp.int32)

    def onward(self, array):
        return lax.ppermute(array, self.axis, self.moves)

    def partner(self, array):
        return lax.ppermute(array, self.axis, self.pairs)

    def total(self, array):
        size = 1
        while size < 2 * self.chips:
            flips = [(i, i ^ size) for i in range(2 * self.chips)]
            array = array + lax.ppermute(array, self.axis, flips)
            size = 2 * size
        return array


class Gather:
    def __init__(self, ring, shard, *deps):
        shard = after(shard, *deps)
        self.ring = ring
        self.rows = shard.shape[0]
        self.half = ring.chips // 2
        self.step = 0
        self.piece = shard
        if ring.plain:
            self.pieces = [lax.all_gather(shard, ring.axis, axis=0, tiled=True)]
            self.step = self.half
            return
        other = ring.partner(shard)
        self.piece = by_core(ring.core, shard, other)
        self.pieces = [self.piece]
        self.echoes = []

    def advance(self, *deps):
        if self.step == self.half:
            return self
        self.step = self.step + 1
        ring, rows = self.ring, self.rows
        piece = after(self.piece, *deps)
        if self.step == self.half:
            piece = lax.dynamic_slice_in_dim(piece, ring.core * rows, rows, 0)
        piece = ring.onward(piece)
        echo = ring.partner(piece)
        self.pieces.append(piece)
        self.echoes.append(echo)
        self.piece = piece
        return self

    def finish(self):
        while self.step < self.half:
            self.advance()
        if self.ring.plain:
            return self.pieces
        return self.pieces[:-1] + self.echoes[:-1] + [self.pieces[-1], self.echoes[-1]]


class Scatter:
    def __init__(self, ring, chunks):
        self.ring = ring
        self.chunks = chunks
        self.half = ring.chips // 2
        self.step = 0 if ring.plain else self.half
        self.arrived = chunks[0]

    def advance(self, *deps):
        if self.step == 0:
            return self
        ring, half, chunks = self.ring, self.half, self.chunks
        if self.step == half:
            echo = ring.partner(chunks[2 * half])
            moving = chunks[2 * half - 1].astype(f32) + echo.astype(f32)
        else:
            echo = ring.partner(chunks[self.step]).astype(f32)
            arrived = self.arrived.astype(f32)
            if self.step == half - 1:
                arrived = spread(ring.core, arrived)
            moving = chunks[half - 1 + self.step].astype(f32) + echo + arrived
        self.arrived = ring.onward(after(moving.astype(bf16), *deps))
        self.step = self.step - 1
        return self

    def finish(self):
        ring = self.ring
        if ring.plain:
            return lax.psum_scatter(
                self.chunks[0].astype(f32), ring.axis, scatter_dimension=0, tiled=True
            )
        while self.step > 0:
            self.advance()
        arrived = self.arrived.astype(f32)
        if self.half == 1:
            arrived = spread(ring.core, arrived)
        own = self.chunks[0].astype(f32) + arrived
        rows = own.shape[0] // 2
        give = lax.dynamic_slice_in_dim(own, (1 - ring.core) * rows, rows, 0).astype(bf16)
        keep = lax.dynamic_slice_in_dim(own, ring.core * rows, rows, 0)
        return keep + ring.partner(give).astype(f32)


def others_of(array, axis):
    count = lax.axis_size(axis)
    received = []
    for shift in range(1, count):
        moves = [(i, (i + shift) % count) for i in range(count)]
        received.append(lax.ppermute(array, axis, moves))
    return received


def by_index(axis, pieces, dim):
    count = lax.axis_size(axis)
    index = lax.axis_index(axis)
    joined = None
    for value in range(count):
        here = jnp.concatenate([pieces[(value - i) % count] for i in range(count)], dim)
        joined = here if joined is None else jnp.where(index == value, here, joined)
    return joined


def gather_rows(array, axis):
    return by_index(axis, [array] + others_of(array, axis), 0)


def scatter_rows(partial, axis):
    count = lax.axis_size(axis)
    index = lax.axis_index(axis)
    rows = partial.shape[0] // count
    total = lax.dynamic_slice_in_dim(partial, index * rows, rows, 0)
    for shift in range(1, count):
        target = (index + shift) % count
        part = lax.dynamic_slice_in_dim(partial, target * rows, rows, 0).astype(bf16)
        moves = [(i, (i + shift) % count) for i in range(count)]
        total = total + lax.ppermute(part, axis, moves).astype(f32)
    return total


def after(array, *done):
    return lax.optimization_barrier((array, *done))[0] if done else array


def split_columns(array, widths):
    pieces = []
    offset = 0
    for width in widths:
        pieces.append(array[:, offset : offset + width])
        offset = offset + width
    return pieces


def on_device(
    tokens, out_cotangent, seq_lengths, norm_gain1, query_weight, key_weight, value_weight,
    out_gate_weight, beta_weight, decay_weight, conv_query, conv_key, conv_value,
    decay_log_rate, decay_bias, out_gain, out_weight, norm_gain2, ffn_gate_weight,
    ffn_up_weight, ffn_down_weight,
):
    ring = Ring("dp")
    local_rows = tokens.shape[0]
    tensor_index = lax.axis_index("tensor")
    seq_length = seq_lengths[0]
    local_pos = tensor_index * local_rows + jnp.arange(local_rows, dtype=jnp.int32)
    local_mask = (local_pos < seq_length).astype(f32)[:, None]
    key_cols = query_weight.shape[1]
    value_cols = value_weight.shape[1]
    heads = beta_weight.shape[1]
    hidden_cols = ffn_gate_weight.shape[1]
    per_step = max(1, heads // 2)
    groups = heads // per_step
    wide_key = key_cols // groups
    wide_value = value_cols // groups
    grouped = 2 * (wide_key + wide_value)

    def group_of(array, group):
        wide = array.shape[1] // groups
        return array[:, group * wide : (group + 1) * wide]

    starts = ring.starts(query_weight.shape[0])
    proj_weights = (query_weight, key_weight, value_weight, out_gate_weight)
    narrow = jnp.concatenate([beta_weight, decay_weight], 1)
    blank = jnp.zeros((narrow.shape[0], LANES - 2 * heads), bf16)
    proj_joined = jnp.concatenate([*proj_weights, narrow, blank, out_weight], 1)
    out_at = proj_joined.shape[1] - value_cols
    ffn_joined = jnp.concatenate([ffn_gate_weight, ffn_up_weight], 1)
    normed1, inverse1, hidden1 = rms_rows(tokens, norm_gain1)
    whole1 = gather_rows(hidden1, "tensor")
    grad_local = (local_mask * out_cotangent.astype(f32)).astype(bf16)
    grad_whole = gather_rows(grad_local, "tensor")
    lanes = jnp.pad(
        jnp.stack([decay_log_rate, decay_bias]), ((0, 0), (heads, LANES - 2 * heads))
    )
    gain_wide = out_gain[None]
    convs = [
        tuple(group_of(conv, group) for conv in (conv_query, conv_key, conv_value))
        for group in range(groups)
    ]

    proj_gather = Gather(ring, proj_joined)
    proj_gather.advance().advance().advance()
    late = proj_gather.piece
    down_pieces = Gather(ring, ffn_down_weight).finish()
    proj_pieces = proj_gather.finish()
    ffn_gather = Gather(ring, ffn_joined, late)
    ffn_pieces = ffn_gather.finish()
    projections = []
    halves = []
    saved = []
    for group in range(groups):
        proj, small, half, *kept = mixer_forward(
            starts, proj_pieces, whole1, lanes, convs[group], gain_wide, heads, group, per_step
        )
        projections.append(proj)
        halves.append(half)
        saved.append(kept)
    partial_branch = branch_rows(starts, proj_pieces, out_at, *halves)
    branch = scatter_rows(partial_branch, "tensor")
    residual = tokens.astype(f32) + branch
    normed2, inverse2, hidden2 = rms_rows(residual, norm_gain2)
    whole2 = gather_rows(hidden2, "tensor")

    inner_act, grad_pre_both, partial_hidden2 = ffn_pass(
        starts, ffn_pieces, down_pieces, whole2, grad_whole
    )
    grad_hidden2 = scatter_rows(partial_hidden2, "tensor")
    ffn_chunks = outer_chunks(
        starts, ffn_pieces, whole2, grad_pre_both, grad_whole, inner_act
    )
    ffn_shard = Scatter(ring, ffn_chunks).finish()
    grad_normed2, second_gain_gradient = rms_back(grad_hidden2, normed2, inverse2, norm_gain2)
    grad_residual = local_mask * out_cotangent.astype(f32) + grad_normed2
    grad_whole1 = gather_rows(grad_residual.astype(bf16), "tensor")
    taken = halves
    conv_grads = []
    gain_sum = 0.0
    scatters = []
    for group in range(groups):
        chunks, conv_grad, (gain_part, carry, lane_sums, partial_hidden) = mixer_backward(
            starts, proj_pieces, whole1, grad_whole1, projections[group], small,
            lanes, convs[group], gain_wide, saved[group], taken, heads, group, per_step,
            group == groups - 1,
        )
        taken = (carry, partial_hidden)
        conv_grads.append(conv_grad)
        gain_sum = gain_sum + gain_part
        scatters.append(Scatter(ring, chunks))
    grad_hidden1 = scatter_rows(partial_hidden, "tensor")
    partial_ffn = branch_rows(
        starts, down_pieces, 0, after(inner_act, partial_hidden)
    )
    ffn_branch = scatter_rows(partial_ffn, "tensor")
    output = (local_mask * (residual + ffn_branch)).astype(bf16)
    grad_normed1, first_gain_gradient = rms_back(grad_hidden1, normed1, inverse1, norm_gain1)
    grad_tokens = (grad_residual + grad_normed1).astype(bf16)
    proj_shards = [scatter.finish() for scatter in scatters]
    edges = [0, wide_key, 2 * wide_key, 2 * wide_key + wide_value, grouped]
    mixer_grads = [
        jnp.concatenate([shard[:, edges[i] : edges[i + 1]] for shard in proj_shards], 1)
        for i in range(4)
    ]
    mixer_grads.append(proj_shards[-1][:, grouped : grouped + heads])
    mixer_grads.append(proj_shards[-1][:, grouped + heads : grouped + 2 * heads])
    ffn_grads = split_columns(ffn_shard, [hidden_cols] * 3)
    grad_conv_query, grad_conv_key, grad_conv_value = [
        jnp.concatenate([conv_grad[i] for conv_grad in conv_grads], 1) for i in range(3)
    ]

    taps = conv_query.shape[0]
    grad_conv_query, grad_conv_key, grad_conv_value, gain_sum, lane_sums = lax.optimization_barrier(
        (grad_conv_query, grad_conv_key, grad_conv_value, gain_sum, lane_sums, grad_hidden1)
    )[:5]
    blocks = [
        jnp.concatenate([grad_conv_query, grad_conv_key], 1),
        grad_conv_value,
        first_gain_gradient[None],
        second_gain_gradient[None],
        gain_sum,
        lane_sums[:, : 2 * heads],
    ]
    wide = max(block.shape[1] for block in blocks)
    tall = sum(block.shape[0] for block in blocks)
    blocks = [jnp.pad(block, ((0, 0), (0, wide - block.shape[1]))) for block in blocks]
    blocks.append(jnp.zeros((-tall % 8, wide), f32))
    packed = ring.total(jnp.concatenate(blocks, 0))
    pieces = [packed] + others_of(packed, "tensor")
    summed = pieces[0]
    for member in pieces[1:]:
        summed = summed + member

    def joined(row, rows, start, cols):
        parts = [member[row : row + rows, start : start + cols] for member in pieces]
        return by_index("tensor", parts, 1)

    gain_row = 2 * taps
    return (
        output,
        grad_tokens,
        summed[gain_row, : norm_gain1.shape[0]],
        mixer_grads[0],
        mixer_grads[1],
        mixer_grads[2],
        mixer_grads[3],
        mixer_grads[4],
        mixer_grads[5],
        joined(0, taps, 0, key_cols),
        joined(0, taps, key_cols, key_cols),
        joined(taps, taps, 0, value_cols),
        joined(gain_row + 3, 1, heads, heads)[0],
        joined(gain_row + 4, 1, heads, heads)[0],
        summed[gain_row + 2, : out_gain.shape[0]],
        proj_shards[0][:, -value_cols:],
        summed[gain_row + 1, : norm_gain2.shape[0]],
        ffn_grads[0],
        ffn_grads[1],
        ffn_grads[2],
    )


def solution(mesh):
    in_specs = (
        P(("dp", "tensor"), None),
        P(("dp", "tensor"), None),
        P("dp"),
        P(),
        P("dp", "tensor"),
        P("dp", "tensor"),
        P("dp", "tensor"),
        P("dp", "tensor"),
        P("dp", "tensor"),
        P("dp", "tensor"),
        P(None, "tensor"),
        P(None, "tensor"),
        P(None, "tensor"),
        P("tensor"),
        P("tensor"),
        P(),
        P("dp", "tensor"),
        P(),
        P("dp", "tensor"),
        P("dp", "tensor"),
        P("dp", "tensor"),
    )
    out_specs = (
        P(("dp", "tensor"), None),
        P(("dp", "tensor"), None),
        P(),
        P("dp", "tensor"),
        P("dp", "tensor"),
        P("dp", "tensor"),
        P("dp", "tensor"),
        P("dp", "tensor"),
        P("dp", "tensor"),
        P(),
        P(),
        P(),
        P(),
        P(),
        P(),
        P("dp", "tensor"),
        P(),
        P("dp", "tensor"),
        P("dp", "tensor"),
        P("dp", "tensor"),
    )

    return jax.shard_map(
        on_device, mesh=mesh, in_specs=in_specs, out_specs=out_specs, check_vma=False
    )
```
